256 devices in a mesh: dp: 8 (over y_hi, x), ctx: 32 (over y_lo, z, core).
Axes of the slice: x: 4, y: 4 (y_hi: 2, y_lo: 2; y = y_hi * 2 + y_lo), z: 8, core: 2. Of those that a mesh axis runs over, the one named last changes fastest.
Arguments:
- queries: bfloat16 [8, 4096, 1024], P('dp', 'ctx'), may hold values from -180 to 180
- keys: bfloat16 [8, 16384, 128], P('dp', 'ctx'), may hold values from -6 to 6
- values: bfloat16 [8, 16384, 128], P('dp', 'ctx'), may hold values from -6 to 6
- grad_out: bfloat16 [8, 4096, 1024], P('dp', 'ctx'), may hold values from -6 to 6
- saved_out: bfloat16 [8, 4096, 1024], P('dp', 'ctx'), may hold values from -1.796875 to 1.796875
- segment_ids: int32 [8, 16384], P('dp', 'ctx'), may hold values from 0 to 127, never falling along the last dimension, each value on 1 to 1024 neighbouring positions
- frame_flags: int32 [8, 128], P('dp'), may hold values 0 or 1
Outputs:
- grad_queries: bfloat16 [8, 4096, 1024], P('dp', 'ctx')
- grad_keys: bfloat16 [8, 16384, 128], P('dp', 'ctx')
- grad_values: bfloat16 [8, 16384, 128], P('dp', 'ctx')
The draws below stay inside these ranges and needn't reach their ends.
All inputs are finite; a program needn't handle non-finite values. No bound on the sum of `frame_flags` on one device may be relied on, other than what follows from the above.
Results may differ from the reference program's by a relative error of at most 0.0051.
Values may be sent and summed in bfloat16 or wider, within the bound.
No kernel may reach another device: no remote copies, remote signals or barrier semaphores. Data moves between devices by JAX's collectives and lax.ppermute only.
A program may use at most 64 MiB of HBM per device.

```python
import math
import jax
import jax.numpy as jnp
import numpy as np
from jax import lax

H = 8
HD = 128
KEY_DEV = 512
Q_DEV = 128
SEQS = 8
SEQ_LEN = 16384
QROWS = 4096
NSEG = 128
SEG_MOST = 1024
N_CTX = 32


def paired_draw(key):
    query_seed = jax.random.fold_in(key, 101)
    key_seed = jax.random.fold_in(key, 202)
    key_field = jnp.clip(jax.random.normal(key_seed, (SEQS, SEQ_LEN, HD), jnp.float32), -6.0, 6.0)
    query_field = jnp.clip(jax.random.normal(query_seed, (SEQS, QROWS, H * HD), jnp.float32), -6.0, 6.0)
    return (query_field, key_field)


def draw_queries(key, part):
    return paired_draw(key)[0].astype(jnp.bfloat16)


def draw_keys(key, part):
    return paired_draw(key)[1].astype(jnp.bfloat16)


def with_ends(values, key, low, top_value):
    dims = values.shape
    place = [jax.random.randint(jax.random.fold_in(key, axis), (), 0, dims[axis]) for axis in range(len(dims))]
    values = values.at[tuple(place)].set(low)
    longest = dims.index(max(dims))
    place[longest] = (place[longest] + 1) % dims[longest]
    return values.at[tuple(place)].set(top_value)


def levels(own_key, extent, pieces, low, largest):
    def one(position, parts):
        heights = jax.random.uniform(jax.random.fold_in(jax.random.fold_in(own_key, 6), position), (parts,), jnp.float32, low / len(pieces), largest / len(pieces))
        return jnp.repeat(jnp.exp(heights), extent[position] // parts).reshape((-1,) + (1,) * (len(extent) - position - 1))

    loudness = one(*pieces[0])
    for cut in pieces[1:]:
        loudness = loudness * one(*cut)
    return loudness


def split_up(count, total, reach, lean):
    loads = [(1 << 20) // math.isqrt(grade ** lean) + 1 for grade in range(2, count + 1)]
    spare, holding = total - reach - (count - 1), [1] * (count - 1)
    while spare > 0:
        candidates = [i for i in range(count - 1) if holding[i] < reach]
        whole, left = sum([loads[i] for i in candidates]), spare
        for i in candidates:
            addition = min(reach - holding[i], max(1, left * loads[i] // whole), spare)
            holding[i] = holding[i] + addition
            spare = spare - addition
    return np.array([reach] + holding)


def uneven_parts(rng, amount, total, reach, skew):
    if amount == 2:
        one = jax.random.randint(rng, (), max(1, total - reach), min(reach, total - 1) + 1)
        return jnp.stack([one, total - one])
    lengths = jnp.asarray(split_up(amount, total, reach, skew), jnp.int32)
    twos = (amount - 1) // 2
    source_of, receiver = lengths[1:1 + 2 * twos:2], lengths[2:2 + 2 * twos:2]
    room = jnp.minimum(source_of - 1, reach - receiver)
    shifted = jax.random.randint(jax.random.fold_in(rng, 1), (twos,), 0, 1 << 20) % (room + 1)
    lengths = lengths.at[1:1 + 2 * twos:2].set(source_of - shifted).at[2:2 + 2 * twos:2].set(receiver + shifted)
    return lengths[jax.random.permutation(jax.random.fold_in(rng, 2), amount)]


def bell_draw(own_key, dims, scale, most, pieces=(), kind=jnp.bfloat16):
    loudness = levels(own_key, dims, pieces, -0.22, 0.18) if pieces else 1.0
    values = jax.random.normal(own_key, dims, jnp.float32) * scale * loudness
    return jnp.minimum(jnp.maximum(values, -most), most).astype(kind)


def setup_inputs(seed: int = 0) -> dict:
    arg_keys = jax.random.split(jax.random.key(seed), 8)
    queries = draw_queries(jax.random.fold_in(arg_keys[7], 71), 0)
    keys = draw_keys(jax.random.fold_in(arg_keys[7], 71), 0)
    values = bell_draw(arg_keys[2], (SEQS, SEQ_LEN, HD), 1.0, 6.0, ((0, 8), (1, 32)))
    grad_out = bell_draw(arg_keys[3], (SEQS, QROWS, H * HD), 1.0, 6.0, ((0, 8), (1, 32)))
    saved_out = bell_draw(arg_keys[4], (SEQS, QROWS, H * HD), 0.3, 1.796875, ((0, 8), (1, 32)))
    segment_ids = jax.vmap(lambda own: jnp.searchsorted(jnp.cumsum(uneven_parts(own, NSEG, SEQ_LEN, SEG_MOST, 2)), jnp.arange(SEQ_LEN), side="right"))(jax.random.split(arg_keys[5], SEQS)).reshape((SEQS, SEQ_LEN)).astype(jnp.int32)
    frame_flags = with_ends((jax.random.randint(arg_keys[6], (SEQS, NSEG), 0, 2) < 1).astype(jnp.int32), jax.random.fold_in(arg_keys[6], 1), 0, 1)
    return {"queries": queries, "keys": keys, "values": values, "grad_out": grad_out, "saved_out": saved_out, "segment_ids": segment_ids, "frame_flags": frame_flags}


def reference(queries, keys, values, grad_out, saved_out, segment_ids, frame_flags):
    score_scale = 1.0 / math.sqrt(HD)
    segment_count = frame_flags.shape[1]

    def one_sequence(operands):
        query_seq, key_seq, value_seq, grad_seq, saved_seq, seg_seq, flag_seq = operands
        onehot = seg_seq[:, None] == jnp.arange(segment_count, dtype=jnp.int32)[None, :]
        frame_of = lax.optimization_barrier(jnp.sum(jnp.where(onehot, flag_seq[None, :], 0), axis=1))
        key_pos = jnp.arange(SEQ_LEN, dtype=jnp.int32)

        def window(carried, rank_index):
            key_grad, value_grad = carried
            row_first = (rank_index * Q_DEV).astype(jnp.int32)
            pos_first = (rank_index * KEY_DEV + KEY_DEV - Q_DEV).astype(jnp.int32)
            query_mat = lax.dynamic_slice_in_dim(query_seq, row_first, Q_DEV, 0).reshape(Q_DEV * H, HD)
            grad_mat = lax.dynamic_slice_in_dim(grad_seq, row_first, Q_DEV, 0)
            saved_mat = lax.dynamic_slice_in_dim(saved_seq, row_first, Q_DEV, 0)
            out_dot = lax.optimization_barrier(jnp.sum((grad_mat.astype(jnp.float32) * saved_mat.astype(jnp.float32)).reshape(Q_DEV * H, HD), axis=1))
            grad_mat = grad_mat.reshape(Q_DEV * H, HD)
            query_pos = pos_first + jnp.arange(Q_DEV, dtype=jnp.int32)
            query_seg = lax.dynamic_slice_in_dim(seg_seq, pos_first, Q_DEV)
            query_frame = lax.dynamic_slice_in_dim(frame_of, pos_first, Q_DEV)
            row_pos = jnp.repeat(query_pos, H)
            row_seg = jnp.repeat(query_seg, H)
            row_frame = jnp.repeat(query_frame, H) == 1
            visible = (key_pos[None, :] <= row_pos[:, None]) | (seg_seq[None, :] == row_seg[:, None]) & row_frame[:, None]
            scores = jnp.dot(query_mat, key_seq.T, preferred_element_type=jnp.float32) * score_scale
            row_top = lax.optimization_barrier(jnp.max(jnp.where(visible, scores, -jnp.inf), axis=1))
            log_total = row_top + jnp.log(lax.optimization_barrier(jnp.sum(jnp.where(visible, jnp.exp(scores - row_top[:, None]), 0.0), axis=1)))
            probs = jnp.where(visible, jnp.exp(scores - log_total[:, None]), 0.0)
            probs_low = probs.astype(jnp.bfloat16)
            dprobs = jnp.dot(grad_mat, value_seq.T, preferred_element_type=jnp.float32)
            dscores = (probs * (dprobs - out_dot[:, None])).astype(jnp.bfloat16)
            query_grad = (score_scale * jnp.dot(dscores, key_seq, preferred_element_type=jnp.float32)).astype(jnp.bfloat16)
            key_grad = key_grad + score_scale * jnp.dot(dscores.T, query_mat, preferred_element_type=jnp.float32)
            value_grad = value_grad + jnp.dot(probs_low.T, grad_mat, preferred_element_type=jnp.float32)
            return ((key_grad, value_grad), query_grad.reshape(Q_DEV, H * HD))
        initial = (jnp.zeros((SEQ_LEN, HD), jnp.float32), jnp.zeros((SEQ_LEN, HD), jnp.float32))
        (key_grad, value_grad), query_grads = lax.scan(window, initial, jnp.arange(N_CTX, dtype=jnp.int32))
        return (query_grads.reshape(QROWS, H * HD), key_grad.astype(jnp.bfloat16), value_grad.astype(jnp.bfloat16))
    grad_queries, grad_keys, grad_values = lax.map(one_sequence, (queries, keys, values, grad_out, saved_out, segment_ids, frame_flags))
    return (grad_queries, grad_keys, grad_values)
```

```python
import functools
import math

import jax
import jax.numpy as jnp
from jax import lax
from jax.experimental import pallas as pl
from jax.experimental.pallas import tpu as pltpu
from jax.sharding import PartitionSpec as P

H = 8
HD = 128
NQ = 128
NK = 512
NZ = 8
SCALE = 1.0 / math.sqrt(HD)
C2 = SCALE * math.log2(math.e)
NEG = -1e30
F32 = jnp.float32
BF16 = jnp.bfloat16
VM = pl.BlockSpec(memory_space=pltpu.VMEM)
SM = pl.BlockSpec(memory_space=pltpu.SMEM)
MIB = 1 << 20


def flip(rho):
    mask = (rho & 1) | ((rho >> 1) << 4)
    return [(i, i ^ mask) for i in range(32)]


def turn(step):
    return [(i, (i // 16) * 16 + (i % 16 + 2 * step) % 16) for i in range(32)]


def behind(step):
    return [(i, (i - step) % 32) for i in range(32)]


def dot_nn(left, right):
    return lax.dot_general(left, right, (((1,), (0,)), ((), ())), preferred_element_type=F32)


def dot_tn(left, right):
    return lax.dot_general(left, right, (((0,), (0,)), ((), ())), preferred_element_type=F32)


def call(body, out, n_in, smem_in=(), scratch=(), vmem=8, flops=0, nbytes=0, alias=None, name=None):
    return pl.pallas_call(
        body,
        out_shape=out,
        in_specs=[SM if i in smem_in else VM for i in range(n_in)],
        out_specs=jax.tree.map(lambda _: VM, out),
        scratch_shapes=list(scratch),
        input_output_aliases=alias or {},
        cost_estimate=pl.CostEstimate(flops=flops, bytes_accessed=nbytes, transcendentals=0),
        compiler_params=pltpu.CompilerParams(vmem_limit_bytes=vmem * MIB),
        name=name,
    )


def shape(dims, dtype=BF16):
    return jax.ShapeDtypeStruct(dims, dtype)


def pack_body(tab, k_ref, v_ref, o0, o1, o2, o3):
    col = tab[1]
    for rho, out in enumerate((o0, o1, o2, o3)):
        first = pl.multiple_of((col ^ rho) * 128, 128)
        out[:, 0:HD] = k_ref[pl.ds(first, 128), :]
        out[:, HD:] = v_ref[pl.ds(first, 128), :]


def aux_body(tab, seg_ref, near_ref, far_ref, flag_ref, grad_ref, saved_ref, out_ref):
    rank = tab[2]
    query = seg_ref[:, NK - NQ :]

    def column(row):
        return jnp.broadcast_to(row, (128, 128)).T

    count = jnp.zeros((128, 128), F32)
    for part in range(4):
        lanes = slice(128 * part, 128 * part + 128)
        count += jnp.where(column(seg_ref[:, lanes]) <= query, 1.0, 0.0)
        count += jnp.where((column(near_ref[:, lanes]) == query) & (rank < 31), 1.0, 0.0)
        count += jnp.where((column(far_ref[:, lanes]) == query) & (rank < 30), 1.0, 0.0)
    last = jnp.sum(count, axis=0, keepdims=True).astype(jnp.int32) + (rank * NK - 1)
    ident = lax.broadcasted_iota(jnp.int32, (128, 128), 0)
    framed = jnp.sum(jnp.where(ident == query, column(flag_ref[...]), 0), axis=0, keepdims=True)
    own = lax.broadcasted_iota(jnp.int32, (1, 128), 1) + (rank * NK + NK - NQ)
    limit = jnp.where(framed == 1, last, own)
    out_ref[...] = jnp.broadcast_to(limit, (16, 128)).astype(F32)
    for h in range(H):
        cols = slice(h * HD, h * HD + HD)
        both = grad_ref[:, cols].astype(F32) * saved_ref[:, cols].astype(F32)
        out_ref[h : h + 1, :] = jnp.sum(both.T, axis=0, keepdims=True)


def turn_body(q0, q1, q2, q3, tall_ref, wide_ref):
    for rho, q in enumerate((q0, q1, q2, q3)):
        for h in range(H):
            tile = q[:, h * HD : h * HD + HD]
            tall_ref[rho, h * NQ : h * NQ + NQ, :] = tile
            wide_ref[rho, :, h * NQ : h * NQ + NQ] = tile.astype(F32).T.astype(BF16)


def item_kind(tab, z_keys, half, rho):
    z, col = tab[0], tab[1]
    own = col ^ rho
    block = 16 * (own >> 1) + 2 * z + (own & 1)
    b0 = col ^ (2 * half)
    b1 = b0 ^ 1
    p0 = (16 * (b0 >> 1) + 2 * z_keys + (b0 & 1)) * NK + 128 * col
    p1 = (16 * (b1 >> 1) + 2 * z_keys + (b1 & 1)) * NK + 128 * col
    full = jnp.maximum(p0, p1) + 127 <= block * NK + NK - NQ
    some = jnp.minimum(p0, p1) <= tab[4 + rho]
    return p0, p1, full, some


def visible_of(p0, p1, limit):
    row = lax.broadcasted_iota(jnp.int32, (256, NQ), 0)
    pos = jnp.where(row < 128, p0 + row, p1 - 128 + row)
    return pos <= limit.astype(jnp.int32)


def stats_body(ks, n_sets, *refs):
    tab, aux_ref, wide_ref, m_in, l_in = refs[:5]
    kvs = refs[5 : 5 + n_sets]
    m_ref, l_ref = refs[5 + n_sets :]
    m_ref[...] = m_in[...]
    l_ref[...] = l_in[...]
    for k, kv in zip(ks, kvs):
        z_keys = (tab[0] + k + NZ) % NZ

        def item(t, _, z_keys=z_keys, kv=kv):
            half, rho = t >> 2, t & 3
            p0, p1, full, some = item_kind(tab, z_keys, half, rho)

            def work(masked):
                keys = kv[pl.ds(pl.multiple_of(half * 256, 256), 256), 0:HD]
                if masked:
                    vis = visible_of(p0, p1, aux_ref[rho, 8:9, :])
                    vis = jnp.concatenate([vis, vis], axis=1)
                for p in range(4):
                    s = dot_nn(keys, wide_ref[rho, :, 256 * p : 256 * p + 256])
                    if masked:
                        s = jnp.where(vis, s, NEG)
                    m_old = jnp.concatenate(
                        [m_ref[rho, 2 * p : 2 * p + 1, :], m_ref[rho, 2 * p + 1 : 2 * p + 2, :]], axis=1
                    )
                    l_old = jnp.concatenate(
                        [l_ref[rho, 2 * p : 2 * p + 1, :], l_ref[rho, 2 * p + 1 : 2 * p + 2, :]], axis=1
                    )
                    m_new = jnp.maximum(m_old, jnp.max(s, axis=0, keepdims=True))
                    e = jnp.exp2((s - m_new) * C2)
                    if masked:
                        e = jnp.where(vis, e, 0.0)
                    l_new = l_old * jnp.exp2((m_old - m_new) * C2) + jnp.sum(e, axis=0, keepdims=True)
                    m_ref[rho, 2 * p : 2 * p + 1, :] = m_new[:, 0:128]
                    m_ref[rho, 2 * p + 1 : 2 * p + 2, :] = m_new[:, 128:256]
                    l_ref[rho, 2 * p : 2 * p + 1, :] = l_new[:, 0:128]
                    l_ref[rho, 2 * p + 1 : 2 * p + 2, :] = l_new[:, 128:256]

            pl.when(full)(lambda: work(False))
            pl.when(jnp.logical_not(full) & some)(lambda: work(True))
            return 0

        lax.fori_loop(0, 8, item, 0)


def grads_body(ks, n_sets, first, *refs):
    n_fixed = 7
    tab, aux_ref, log_ref, qw_ref, qt_ref, gw_ref, gt_ref = refs[:n_fixed]
    kvs = refs[n_fixed : n_fixed + n_sets]
    rest = refs[n_fixed + n_sets :]
    if first:
        dq_in, rest = None, rest
    else:
        dq_in, rest = rest[0], rest[1:]
    dq_ref = rest[0]
    outs = rest[1 : 1 + n_sets]
    p_all, d_all = rest[1 + n_sets :]
    if first:
        dq_ref[...] = jnp.zeros_like(dq_ref)
    else:
        dq_ref[...] = dq_in[...]
    for k, kv, out in zip(ks, kvs, outs):
        z_keys = (tab[0] + k + NZ) % NZ
        out[...] = jnp.zeros_like(out)

        def item(t, _, z_keys=z_keys, kv=kv, out=out):
            half, rho = t >> 2, t & 3
            p0, p1, full, some = item_kind(tab, z_keys, half, rho)

            def work(masked):
                rows = pl.ds(pl.multiple_of(half * 256, 256), 256)
                keys = kv[rows, 0:HD]
                vals = kv[rows, HD:]
                if masked:
                    vis = visible_of(p0, p1, aux_ref[rho, 8:9, :])
                    vis = jnp.concatenate([vis, vis], axis=1)
                for p in range(4):
                    cols = slice(256 * p, 256 * p + 256)
                    total = jnp.concatenate(
                        [log_ref[rho, 2 * p : 2 * p + 1, :], log_ref[rho, 2 * p + 1 : 2 * p + 2, :]], axis=1
                    )
                    mean = jnp.concatenate(
                        [aux_ref[rho, 2 * p : 2 * p + 1, :], aux_ref[rho, 2 * p + 1 : 2 * p + 2, :]], axis=1
                    )
                    s = dot_nn(keys, qw_ref[rho, :, cols])
                    dp = dot_nn(vals, gw_ref[rho, :, cols])
                    prob = jnp.exp2((s - total) * C2)
                    if masked:
                        prob = jnp.where(vis, prob, 0.0)
                    p_all[:, cols] = prob.astype(BF16)
                    d_all[:, cols] = (prob * (dp - mean)).astype(BF16)
                d = d_all[...]
                out[rows, 0:HD] += dot_nn(d, qt_ref[rho])
                out[rows, HD:] += dot_nn(p_all[...], gt_ref[rho])
                dq_ref[rho] += dot_tn(keys, d)

            pl.when(full)(lambda: work(False))
            pl.when(jnp.logical_not(full) & some)(lambda: work(True))
            return 0

        lax.fori_loop(0, 8, item, 0)


def emit_body(dq_ref, o0, o1, o2, o3):
    for rho, out in enumerate((o0, o1, o2, o3)):
        for h in range(H):
            tile = dq_ref[rho, :, h * NQ : h * NQ + NQ]
            out[:, h * HD : h * HD + HD] = (tile.T * SCALE).astype(BF16)


def place_body(tab, a0, a1, a2, a3, q0, q1, q2, q3, gq_ref, gk_ref, gv_ref):
    col = tab[1]
    for rho, part in enumerate((a0, a1, a2, a3)):
        rows = pl.ds(pl.multiple_of((col ^ rho) * 128, 128), 128)
        gk_ref[rows, :] = part[:, 0:HD]
        gv_ref[rows, :] = part[:, HD:]
    total = q0[...].astype(F32) + q1[...].astype(F32) + q2[...].astype(F32) + q3[...].astype(F32)
    gq_ref[...] = total.astype(BF16)


def per_device(queries, keys, values, grad_out, saved_out, segment_ids, frame_flags):
    hop = functools.partial(lax.ppermute, axis_name="ctx")
    rank = lax.axis_index("ctx").astype(jnp.int32)
    z = (rank % 16) // 2
    col = 2 * (rank // 16) + rank % 2
    tab0 = jnp.stack([z, col, rank, rank])
    near = hop(segment_ids, perm=behind(1))
    far = hop(segment_ids, perm=behind(2))

    parts = call(pack_body, [shape((128, 256))] * 4, 3, (0,), nbytes=MIB, name="pack")(
        tab0, keys[0], values[0]
    )
    own_set = jnp.concatenate([parts[0]] + [hop(parts[r], perm=flip(r)) for r in (1, 2, 3)], axis=0)

    def four(x):
        other = hop(x, perm=flip(2))
        return (x, hop(x, perm=flip(1)), other, hop(other, perm=flip(1)))

    q_four = four(queries[0])
    aux_own = call(aux_body, shape((16, 128), F32), 7, (0,), nbytes=MIB, name="aux")(
        tab0, segment_ids, near, far, frame_flags, grad_out[0], saved_out[0]
    )
    aux = jnp.stack([aux_own] + [hop(aux_own, perm=flip(r)) for r in (1, 2, 3)])
    tab = jnp.concatenate([tab0, jnp.max(aux[:, 8, :], axis=1).astype(jnp.int32)])
    sets = {0: own_set}
    fwd = bwd = own_set
    for k in (1, 2, 3):
        fwd = sets[-k] = hop(fwd, perm=turn(1))
        bwd = sets[k] = hop(bwd, perm=turn(-1))
    sets[4] = hop(bwd, perm=turn(-1))
    g_four = four(grad_out[0])

    forms = [shape((4, NQ * H, HD)), shape((4, HD, NQ * H))]
    q_tall, q_wide = call(turn_body, forms, 4, vmem=16, nbytes=4 * MIB, name="turn_q")(*q_four)
    stat = shape((4, H, NQ), F32)
    m = jnp.full((4, H, NQ), NEG, F32)
    l = jnp.zeros((4, H, NQ), F32)
    for ks in ((0,), (1, -1), (2, -2), (3, -3), (4,)):
        n = len(ks)
        m, l = call(
            functools.partial(stats_body, ks, n), [stat, stat], 5 + n, (0,), vmem=16,
            flops=n * (1 << 29), nbytes=2 * MIB, name=f"stats{ks[0]}",
        )(tab, aux, q_wide, m, l, *[sets[k] for k in ks])
    g_tall, g_wide = call(turn_body, forms, 4, vmem=16, nbytes=4 * MIB, name="turn_g")(*g_four)

    ml = jnp.stack([m, l])
    tops, sums = [m], [l]
    for r in (1, 2, 3):
        got = hop(ml, perm=flip(r))
        order = [rho ^ r for rho in range(4)]
        tops.append(jnp.stack([got[0, o] for o in order]))
        sums.append(jnp.stack([got[1, o] for o in order]))
    top = functools.reduce(jnp.maximum, tops)
    total = sum(s * jnp.exp2((t - top) * C2) for s, t in zip(sums, tops))
    log_total = top + jnp.log2(total) * (1.0 / C2)

    dq = None
    up = down = None
    acc = shape((NK, 2 * HD), F32)
    dq_shape = shape((4, HD, NQ * H), F32)
    for ks in ((4,), (3, -3), (2, -2), (1, -1), (0,)):
        n = len(ks)
        first = dq is None
        args = [tab, aux, log_total, q_wide, q_tall, g_wide, g_tall] + [sets[k] for k in ks]
        args += [] if first else [dq]
        dq, *adds = call(
            functools.partial(grads_body, ks, n, first), [dq_shape] + [acc] * n, len(args), (0,),
            scratch=[pltpu.VMEM((256, NQ * H), BF16)] * 2, vmem=24,
            flops=n * 5 * (1 << 29), nbytes=8 * MIB,
            alias={} if first else {len(args) - 1: 0}, name=f"grads{ks[0]}",
        )(*args)
        if ks[0] == 0:
            own = adds[0] + up.astype(F32) + down.astype(F32)
            break
        send_up = adds[0] if up is None else adds[0] + up.astype(F32)
        up = hop(send_up.astype(BF16), perm=turn(1))
        if n == 2:
            send_down = adds[1] if down is None else adds[1] + down.astype(F32)
            down = hop(send_down.astype(BF16), perm=turn(-1))
    scales = jnp.where(jnp.arange(2 * HD) < HD, SCALE, 1.0).astype(F32)
    own = (own * scales[None, :]).astype(BF16)
    dq_four = call(emit_body, [shape((NQ, H * HD))] * 4, 1, vmem=16, nbytes=3 * MIB, name="emit")(dq)
    q_back = [dq_four[0]] + [hop(dq_four[r], perm=flip(r)) for r in (1, 2, 3)]
    a_back = [own[0:128]] + [hop(own[128 * r : 128 * r + 128], perm=flip(r)) for r in (1, 2, 3)]
    gq, gk, gv = call(
        place_body, [shape((NQ, H * HD)), shape((NK, HD)), shape((NK, HD))], 9, (0,), nbytes=2 * MIB,
        name="place",
    )(tab0, *a_back, *q_back)
    return gq[None], gk[None], gv[None]


def solution(mesh):
    row = P("dp", "ctx", None)
    return jax.shard_map(
        per_device,
        mesh=mesh,
        in_specs=(row, row, row, row, row, P("dp", "ctx"), P("dp", None)),
        out_specs=(row, row, row),
        check_vma=False,
    )
```

```python
import functools
import math

import jax
import jax.numpy as jnp
from jax import lax
from jax.experimental import pallas as pl
from jax.experimental.pallas import tpu as pltpu
from jax.sharding import PartitionSpec as P

H = 8
HD = 128
NQ = 128
NK = 512
NZ = 8
SCALE = 1.0 / math.sqrt(HD)
C2 = SCALE * math.log2(math.e)
NEG = -1e30
F32 = jnp.float32
BF16 = jnp.bfloat16
VM = pl.BlockSpec(memory_space=pltpu.VMEM)
SM = pl.BlockSpec(memory_space=pltpu.SMEM)
MIB = 1 << 20


def flip(rho):
    mask = (rho & 1) | ((rho >> 1) << 4)
    return [(i, i ^ mask) for i in range(32)]


def turn(step):
    return [(i, (i // 16) * 16 + (i % 16 + 2 * step) % 16) for i in range(32)]


def behind(step):
    return [(i, (i - step) % 32) for i in range(32)]


def dot_nn(left, right):
    return lax.dot_general(left, right, (((1,), (0,)), ((), ())), preferred_element_type=F32)


def dot_tn(left, right):
    return lax.dot_general(left, right, (((0,), (0,)), ((), ())), preferred_element_type=F32)


def call(body, out, specs, scratch=(), vmem=8, flops=0, nbytes=0, alias=None, name=None):
    return pl.pallas_call(
        body,
        out_shape=out,
        in_specs=specs,
        out_specs=jax.tree.map(lambda _: VM, out),
        scratch_shapes=list(scratch),
        input_output_aliases=alias or {},
        cost_estimate=pl.CostEstimate(flops=flops, bytes_accessed=nbytes, transcendentals=0),
        compiler_params=pltpu.CompilerParams(vmem_limit_bytes=vmem * MIB),
        name=name,
    )


def shape(dims, dtype=BF16):
    return jax.ShapeDtypeStruct(dims, dtype)


def column(row):
    return jnp.broadcast_to(row, (128, 128)).T


def begin_body(tab, k_hbm, v_hbm, seg_hbm, flag_hbm, q_hbm, o0, o1, o2, o3, q_out, k_ref, v_ref, seg_ref, flag_ref, sems):
    moves = [
        pltpu.make_async_copy(source, target, sems.at[n])
        for n, (source, target) in enumerate(
            [(seg_hbm, seg_ref), (flag_hbm, flag_ref), (k_hbm, k_ref), (v_hbm, v_ref), (q_hbm, q_out.at[0:NQ, :])]
        )
    ]
    for move in moves:
        move.start()
    moves[0].wait()
    moves[1].wait()
    own = seg_ref[:, NK - NQ :]
    ident = lax.broadcasted_iota(jnp.int32, (128, 128), 0)
    framed = jnp.sum(jnp.where(ident == own, column(flag_ref[...]), 0), axis=0, keepdims=True)
    tag = jnp.where(framed == 1, own, -1).astype(F32)
    q_out[NQ:, :] = jnp.broadcast_to(jnp.concatenate([tag] * H, axis=1), (16, H * HD)).astype(BF16)
    moves[2].wait()
    moves[3].wait()
    for rho, out in enumerate((o0, o1, o2, o3)):
        first = pl.multiple_of((tab[1] ^ rho) * 128, 128)
        out[0:128, 0:HD] = k_ref[pl.ds(first, 128), :]
        out[0:128, HD:] = v_ref[pl.ds(first, 128), :]
        seg = seg_ref[:, pl.ds(first, 128)].astype(F32)
        out[128:, :] = jnp.broadcast_to(jnp.concatenate([seg, seg], axis=1), (16, 256)).astype(BF16)
    moves[4].wait()


def join_body(p0, p1, p2, p3, out):
    row = lax.broadcasted_iota(jnp.int32, (16, 256), 0)
    seg = jnp.zeros((16, 256), F32)
    for rho, part in enumerate((p0, p1, p2, p3)):
        out[128 * rho : 128 * rho + 128, :] = part[0:128, :]
        seg = jnp.where(row == rho, part[128:, :].astype(F32), seg)
    out[NK:, :] = seg.astype(BF16)


def cotangent_body(g_ref, saved_ref, out_ref):
    out_ref[0:NQ, :] = g_ref[...]
    row = lax.broadcasted_iota(jnp.int32, (16, HD), 0)
    for h in range(H):
        cols = slice(h * HD, h * HD + HD)
        both = g_ref[:, cols].astype(F32) * saved_ref[:, cols].astype(F32)
        mean = jnp.sum(both.T, axis=0, keepdims=True)
        top = mean.astype(BF16).astype(F32)
        mid = (mean - top).astype(BF16).astype(F32)
        low = mean - top - mid
        out_ref[NQ:, cols] = jnp.where(row == 0, top, jnp.where(row == 1, mid, low)).astype(BF16)


def turn_body(pieces, q0, q1, q2, q3, tall_ref, wide_ref, row_ref):
    for rho, q in enumerate((q0, q1, q2, q3)):
        for h in range(H):
            tile = q[0:NQ, h * HD : h * HD + HD]
            tall_ref[rho, h * NQ : h * NQ + NQ, :] = tile
            wide_ref[rho, :, h * NQ : h * NQ + NQ] = tile.astype(F32).T.astype(BF16)
        extra = q[NQ:, :].astype(F32)
        row = extra[0:1, :]
        for n in range(1, pieces):
            row = row + extra[n : n + 1, :]
        row_ref[rho] = row


def item_kind(tab, z_keys, half, rho):
    z, col = tab[0], tab[1]
    own = col ^ rho
    block = 16 * (own >> 1) + 2 * z + (own & 1)
    b0 = col ^ (2 * half)
    b1 = b0 ^ 1
    p0 = (16 * (b0 >> 1) + 2 * z_keys + (b0 & 1)) * NK + 128 * col
    p1 = (16 * (b1 >> 1) + 2 * z_keys + (b1 & 1)) * NK + 128 * col
    first = block * NK + NK - NQ
    full = jnp.maximum(p0, p1) + 127 <= first
    some = jnp.minimum(p0, p1) <= first + NQ - 1 + 1023
    return p0, p1, first, full, some


def visible_of(kv, n, half, p0, p1, first, tag):
    row = lax.broadcasted_iota(jnp.int32, (128, NQ), 0)
    query = lax.broadcasted_iota(jnp.int32, (128, NQ), 1) + first
    seg = kv[n, NK:, 0:128].astype(F32)
    which = lax.broadcasted_iota(jnp.int32, (16, 128), 0)
    parts = []
    for c, p in enumerate((p0, p1)):
        line = jnp.sum(jnp.where(which == 2 * half + c, seg, 0.0), axis=0, keepdims=True)
        parts.append(jnp.where((p + row <= query) | (column(line) == tag), 1.0, 0.0))
    both = jnp.concatenate(parts, axis=0)
    return jnp.concatenate([both, both], axis=1) > 0.5


def items(ks, tab, kv, body):
    def item(t, _):
        n, half, rho = t >> 3, (t >> 2) & 1, t & 3
        k = ks[0] if len(ks) == 1 else jnp.where(n == 0, ks[0], ks[1])
        z_keys = (tab[0] + k + NZ) & (NZ - 1)
        kind = item_kind(tab, z_keys, half, rho)
        full, some = kind[3:]
        pl.when(full)(lambda: body(n, half, rho, kind, False))
        if 0 in ks or 1 in ks:
            pl.when(jnp.logical_not(full) & some)(lambda: body(n, half, rho, kind, True))
        return 0

    lax.fori_loop(0, 8 * len(ks), item, 0)


def stats_body(ks, *refs):
    n_sets = len(ks)
    tab, tag_ref, wide_ref, m_in, l_in = refs[:5]
    kvs, (m_ref, l_ref, kv) = refs[5 : 5 + n_sets], refs[5 + n_sets :]
    m_ref[...] = m_in[...]
    l_ref[...] = l_in[...]
    for n in range(n_sets):
        kv[n] = kvs[n][...]

    def body(n, half, rho, kind, masked):
        keys = kv[n, pl.ds(pl.multiple_of(half * 256, 256), 256), 0:HD]
        if masked:
            vis = visible_of(kv, n, half, *kind[:3], tag_ref[rho, :, 0:128])
        for p in range(4):
            cols = slice(256 * p, 256 * p + 256)
            s = dot_nn(keys, wide_ref[rho, :, cols])
            if masked:
                s = jnp.where(vis, s, NEG)
            m_old = m_ref[rho, :, cols]
            m_new = jnp.maximum(m_old, jnp.max(s, axis=0, keepdims=True))
            e = jnp.exp2((s - m_new) * C2)
            if masked:
                e = jnp.where(vis, e, 0.0)
            l_ref[rho, :, cols] = l_ref[rho, :, cols] * jnp.exp2((m_old - m_new) * C2) + jnp.sum(
                e, axis=0, keepdims=True
            )
            m_ref[rho, :, cols] = m_new

    items(ks, tab, kv, body)


def grads_body(ks, first, *refs):
    n_sets = len(ks)
    tab, tag_ref, mean_ref, log_ref, qw_ref, qt_ref, gw_ref, gt_ref = refs[:8]
    kvs, rest = refs[8 : 8 + n_sets], refs[8 + n_sets :]
    if first:
        dq_ref, rest = rest[0], rest[1:]
        dq_ref[...] = jnp.zeros_like(dq_ref)
    else:
        dq_ref, rest = rest[1], (rest[0],) + rest[2:]
        dq_ref[...] = rest[0][...]
        rest = rest[1:]
    outs, (kv, acc, p_all, d_all) = rest[:n_sets], rest[n_sets:]
    for n in range(n_sets):
        kv[n] = kvs[n][...]
    acc[...] = jnp.zeros_like(acc)

    def body(n, half, rho, kind, masked):
        rows = pl.ds(pl.multiple_of(half * 256, 256), 256)
        keys = kv[n, rows, 0:HD]
        vals = kv[n, rows, HD:]
        if masked:
            vis = visible_of(kv, n, half, *kind[:3], tag_ref[rho, :, 0:128])
        for p in range(4):
            cols = slice(256 * p, 256 * p + 256)
            s = dot_nn(keys, qw_ref[rho, :, cols])
            dp = dot_nn(vals, gw_ref[rho, :, cols])
            prob = jnp.exp2((s - log_ref[rho, :, cols]) * C2)
            if masked:
                prob = jnp.where(vis, prob, 0.0)
            p_all[:, cols] = prob.astype(BF16)
            d_all[:, cols] = (prob * (dp - mean_ref[rho, :, cols])).astype(BF16)
        d = d_all[...]
        acc[n, rows, 0:HD] += dot_nn(d, qt_ref[rho])
        acc[n, rows, HD:] += dot_nn(p_all[...], gt_ref[rho])
        dq_ref[rho] += dot_tn(keys, d)

    items(ks, tab, kv, body)
    for n in range(n_sets):
        outs[n][...] = acc[n]


def emit_body(dq_ref, o0, o1, o2, o3):
    for rho, out in enumerate((o0, o1, o2, o3)):
        for h in range(H):
            tile = dq_ref[rho, :, h * NQ : h * NQ + NQ]
            out[:, h * HD : h * HD + HD] = (tile.T * SCALE).astype(BF16)


def place_body(tab, a0, a1, a2, a3, q0, q1, q2, gq_ref, gk_ref, gv_ref):
    col = tab[1]
    for rho, part in enumerate((a0, a1, a2, a3)):
        rows = pl.ds(pl.multiple_of((col ^ rho) * 128, 128), 128)
        gk_ref[rows, :] = part[:, 0:HD]
        gv_ref[rows, :] = part[:, HD:]
    total = q0[...].astype(F32) + q1[...].astype(F32) + q2[...].astype(F32)
    gq_ref[...] = total.astype(BF16)


def per_device(queries, keys, values, grad_out, saved_out, segment_ids, frame_flags):
    hop = functools.partial(lax.ppermute, axis_name="ctx")
    rank = lax.axis_index("ctx").astype(jnp.int32)
    tab = jnp.stack([(rank >> 1) & 7, 2 * (rank >> 4) + (rank & 1)])
    hbm = pl.BlockSpec(memory_space=pltpu.HBM)

    *parts, q_own = call(
        begin_body, [shape((144, 256))] * 4 + [shape((NQ + 16, H * HD))], [SM] + [hbm] * 5, nbytes=MIB,
        scratch=[
            pltpu.VMEM((NK, HD), BF16), pltpu.VMEM((NK, HD), BF16), pltpu.VMEM((1, NK), jnp.int32),
            pltpu.VMEM((1, 128), jnp.int32), pltpu.SemaphoreType.DMA((5,)),
        ],
        vmem=58, name="begin",
    )(tab, keys[0], values[0], segment_ids, frame_flags, queries[0])
    got = [hop(parts[r], perm=flip(r)) for r in (1, 2, 3)]
    own_set = call(join_body, shape((NK + 16, 256)), [VM] * 4, nbytes=MIB, name="join")(parts[0], *got)

    def four(x):
        other = hop(x, perm=flip(2))
        return (x, hop(x, perm=flip(1)), other, hop(other, perm=flip(1)))

    q_four = four(q_own)
    g_own = call(cotangent_body, shape((NQ + 16, H * HD)), [VM] * 2, nbytes=MIB, name="cotangent")(
        grad_out[0], saved_out[0]
    )
    forms = [shape((4, NQ * H, HD)), shape((4, HD, NQ * H)), shape((4, 1, NQ * H), F32)]

    def turned(four_of, pieces, name):
        return call(
            functools.partial(turn_body, pieces), forms, [VM] * 4, vmem=16, nbytes=4 * MIB, name=name
        )(*four_of)

    q_tall, q_wide, tag = turned(q_four, 1, "turn_q")
    stat = shape((4, 1, NQ * H), F32)
    m = jnp.full((4, 1, NQ * H), NEG, F32)
    l = jnp.zeros((4, 1, NQ * H), F32)
    sets = {0: own_set}
    fwd = bwd = own_set
    for step in range(5):
        ks = (0,) if step == 0 else (4,) if step == 4 else (step, -step)
        n = len(ks)
        if step < 3:
            fwd, bwd = hop(fwd, perm=turn(1)), hop(bwd, perm=turn(-1))
        elif step == 3:
            bwd = hop(bwd, perm=turn(-1))
        m, l = call(
            functools.partial(stats_body, ks), [stat, stat], [SM] + [VM] * (4 + n), vmem=16,
            scratch=[pltpu.VMEM((n, NK + 16, 256), BF16)], flops=n * (1 << 29), nbytes=2 * MIB,
            name=f"stats{ks[0]}",
        )(tab, tag, q_wide, m, l, *[sets[k] for k in ks])
        if step < 4:
            fwd, bwd, m, l = lax.optimization_barrier((fwd, bwd, m, l))
            sets[step + 1] = bwd
            if step < 3:
                sets[-step - 1] = fwd
        if step == 0:
            g_four = four(g_own)
    g_tall, g_wide, mean = turned(g_four, 3, "turn_g")

    ml = jnp.concatenate([m, l], axis=0)
    tops, sums = [m], [l]
    for r in (1, 2, 3):
        got = hop(ml, perm=flip(r))
        tops.append(jnp.concatenate([got[rho ^ r : (rho ^ r) + 1] for rho in range(4)], axis=0))
        sums.append(jnp.concatenate([got[4 + (rho ^ r) : 5 + (rho ^ r)] for rho in range(4)], axis=0))
    top = functools.reduce(jnp.maximum, tops)
    total = sum(s * jnp.exp2((t - top) * C2) for s, t in zip(sums, tops))
    log_total = top + jnp.log2(total) * (1.0 / C2)

    dq = None
    up = down = None
    acc = shape((NK, 2 * HD), F32)
    dq_shape = shape((4, HD, NQ * H), F32)
    for ks in ((4,), (3, -3), (2, -2), (1, -1), (0,)):
        n = len(ks)
        first = dq is None
        args = [tab, tag, mean, log_total, q_wide, q_tall, g_wide, g_tall] + [sets[k] for k in ks]
        args += [] if first else [dq]
        dq, *adds = call(
            functools.partial(grads_body, ks, first), [dq_shape] + [acc] * n,
            [SM] + [VM] * (len(args) - 1),
            scratch=[pltpu.VMEM((n, NK + 16, 256), BF16), pltpu.VMEM((n, NK, 256), F32)]
            + [pltpu.VMEM((256, NQ * H), BF16)] * 2,
            vmem=24, flops=n * 5 * (1 << 29), nbytes=8 * MIB,
            alias={} if first else {len(args) - 1: 0}, name=f"grads{ks[0]}",
        )(*args)
        if ks[0] == 0:
            own = adds[0] + up.astype(F32) + down.astype(F32)
            break
        sends = [(adds[0] if up is None else adds[0] + up.astype(F32)).astype(BF16)]
        if n == 2:
            sends.append((adds[1] if down is None else adds[1] + down.astype(F32)).astype(BF16))
        dq, *sends = lax.optimization_barrier((dq, *sends))
        up = hop(sends[0], perm=turn(1))
        if n == 2:
            down = hop(sends[1], perm=turn(-1))
    scales = jnp.where(jnp.arange(2 * HD) < HD, SCALE, 1.0).astype(F32)
    own = (own * scales[None, :]).astype(BF16)
    dq_four = call(emit_body, [shape((NQ, H * HD))] * 4, [VM], vmem=16, nbytes=3 * MIB, name="emit")(dq)
    across = dq_four[2].astype(F32) + hop(dq_four[3], perm=flip(1)).astype(F32)
    q_back = [dq_four[0], hop(dq_four[1], perm=flip(1)), hop(across.astype(BF16), perm=flip(2))]
    a_back = [own[0:128]] + [hop(own[128 * r : 128 * r + 128], perm=flip(r)) for r in (1, 2, 3)]
    gq, gk, gv = call(
        place_body, [shape((NQ, H * HD)), shape((NK, HD)), shape((NK, HD))], [SM] + [VM] * 7,
        nbytes=2 * MIB, name="place",
    )(tab, *a_back, *q_back)
    return gq[None], gk[None], gv[None]


def solution(mesh):
    row = P("dp", "ctx", None)
    return jax.shard_map(
        per_device,
        mesh=mesh,
        in_specs=(row, row, row, row, row, P("dp", "ctx"), P("dp", None)),
        out_specs=(row, row, row),
        check_vma=False,
    )
```

```python
import functools
import math

import jax
import jax.numpy as jnp
from jax import lax
from jax.experimental import pallas as pl
from jax.experimental.pallas import tpu as pltpu
from jax.sharding import PartitionSpec as P


H = 8
HD = 128
NQ = 128
NK = 512
NZ = 8
SCALE = 1.0 / math.sqrt(HD)
C2 = SCALE * math.log2(math.e)
NEG = -1e30
F32 = jnp.float32
BF16 = jnp.bfloat16
VM = pl.BlockSpec(memory_space=pltpu.VMEM)
SM = pl.BlockSpec(memory_space=pltpu.SMEM)
MIB = 1 << 20


def flip(rho):
    mask = (rho & 1) | ((rho >> 1) << 4)
    return [(i, i ^ mask) for i in range(32)]


def turn(step):
    return [(i, (i // 16) * 16 + (i % 16 + 2 * step) % 16) for i in range(32)]


def dot_nn(left, right):
    return lax.dot_general(left, right, (((1,), (0,)), ((), ())), preferred_element_type=F32)


def dot_tn(left, right):
    return lax.dot_general(left, right, (((0,), (0,)), ((), ())), preferred_element_type=F32)


def call(body, out, specs, scratch=(), vmem=8, flops=0, nbytes=0, alias=None):
    return pl.pallas_call(
        body,
        out_shape=out,
        in_specs=specs,
        out_specs=jax.tree.map(lambda _: VM, out),
        scratch_shapes=list(scratch),
        input_output_aliases=alias or {},
        cost_estimate=pl.CostEstimate(flops=flops, bytes_accessed=nbytes, transcendentals=0),
        compiler_params=pltpu.CompilerParams(vmem_limit_bytes=vmem * MIB),
    )


def shape(dims, dtype=BF16):
    return jax.ShapeDtypeStruct(dims, dtype)


def each(count, body):
    lax.fori_loop(0, count, lambda t, _: (body(t), 0)[1], 0)


def lanes(t):
    return pl.ds(pl.multiple_of(t * 128, 128), 128)


def take_sets(kv, kvs):
    def rows(t):
        part = pl.ds(pl.multiple_of(t * 48, 16), 48)
        for n in range(len(kvs)):
            kv[n, part, :] = kvs[n][part, :]

    each(11, rows)


def column(row):
    return jnp.broadcast_to(row, (128, 128)).T


def begin_body(tab, k_hbm, v_hbm, seg_hbm, flag_hbm, q_hbm, o0, o1, o2, o3, q_out, k_ref, v_ref, seg_ref, flag_ref, sems):
    moves = [
        pltpu.make_async_copy(source, target, sems.at[n])
        for n, (source, target) in enumerate(
            [(seg_hbm, seg_ref), (flag_hbm, flag_ref), (k_hbm, k_ref), (v_hbm, v_ref), (q_hbm, q_out.at[0:NQ, :])]
        )
    ]
    for move in moves:
        move.start()
    moves[0].wait()
    moves[1].wait()
    own = seg_ref[:, NK - NQ :]
    ident = lax.broadcasted_iota(jnp.int32, (128, 128), 0)
    framed = jnp.sum(jnp.where(ident == own, column(flag_ref[...]), 0), axis=0, keepdims=True)
    tag = jnp.where(framed == 1, own, -1).astype(F32)
    q_out[NQ:, :] = jnp.broadcast_to(jnp.concatenate([tag] * H, axis=1), (16, H * HD)).astype(BF16)
    moves[2].wait()
    moves[3].wait()
    for rho, out in enumerate((o0, o1, o2, o3)):
        first = pl.multiple_of((tab[1] ^ rho) * 128, 128)
        out[0:128, 0:HD] = k_ref[pl.ds(first, 128), :]
        out[0:128, HD:] = v_ref[pl.ds(first, 128), :]
        seg = seg_ref[:, pl.ds(first, 128)].astype(F32)
        out[128:, :] = jnp.broadcast_to(jnp.concatenate([seg, seg], axis=1), (16, 256)).astype(BF16)
    moves[4].wait()


def join_body(p0, p1, p2, p3, out):
    row = lax.broadcasted_iota(jnp.int32, (16, 256), 0)
    seg = jnp.zeros((16, 256), F32)
    for rho, part in enumerate((p0, p1, p2, p3)):
        out[128 * rho : 128 * rho + 128, :] = part[0:128, :]
        seg = jnp.where(row == rho, part[128:, :].astype(F32), seg)
    out[NK:, :] = seg.astype(BF16)


def cotangent_body(g_ref, saved_ref, out_ref):
    out_ref[0:NQ, :] = g_ref[...]
    row = lax.broadcasted_iota(jnp.int32, (16, HD), 0)
    for h in range(H):
        cols = slice(h * HD, h * HD + HD)
        both = g_ref[:, cols].astype(F32) * saved_ref[:, cols].astype(F32)
        mean = jnp.sum(both.T, axis=0, keepdims=True)
        top = mean.astype(BF16).astype(F32)
        mid = (mean - top).astype(BF16).astype(F32)
        low = mean - top - mid
        out_ref[NQ:, cols] = jnp.where(row == 0, top, jnp.where(row == 1, mid, low)).astype(BF16)


def turn_body(pieces, q0, q1, q2, q3, tall_ref, wide_ref, row_ref):
    def head(h):
        for rho, q in enumerate((q0, q1, q2, q3)):
            tile = q[0:NQ, lanes(h)]
            tall_ref[rho, lanes(h), :] = tile
            wide_ref[rho, :, lanes(h)] = tile.astype(F32).T.astype(BF16)

    each(H, head)
    for rho, q in enumerate((q0, q1, q2, q3)):
        extra = q[NQ:, :].astype(F32)
        row = extra[0:1, :]
        for n in range(1, pieces):
            row = row + extra[n : n + 1, :]
        row_ref[rho] = row


def item_kind(tab, z_keys, half, rho):
    z, col = tab[0], tab[1]
    own = col ^ rho
    block = 16 * (own >> 1) + 2 * z + (own & 1)
    b0 = col ^ (2 * half)
    b1 = b0 ^ 1
    p0 = (16 * (b0 >> 1) + 2 * z_keys + (b0 & 1)) * NK + 128 * col
    p1 = (16 * (b1 >> 1) + 2 * z_keys + (b1 & 1)) * NK + 128 * col
    first = block * NK + NK - NQ
    full = jnp.maximum(p0, p1) + 127 <= first
    some = jnp.minimum(p0, p1) <= first + NQ - 1 + 1023
    return p0, p1, first, full, some


def visible_of(kv, n, half, p0, p1, first, tag):
    row = lax.broadcasted_iota(jnp.int32, (128, NQ), 0)
    query = lax.broadcasted_iota(jnp.int32, (128, NQ), 1) + first
    seg = kv[n, NK:, 0:128].astype(F32)
    which = lax.broadcasted_iota(jnp.int32, (16, 128), 0)
    parts = []
    for c, p in enumerate((p0, p1)):
        line = jnp.sum(jnp.where(which == 2 * half + c, seg, 0.0), axis=0, keepdims=True)
        parts.append(jnp.where((p + row <= query) | (column(line) == tag), 1.0, 0.0))
    both = jnp.concatenate(parts, axis=0)
    return jnp.concatenate([both, both], axis=1) > 0.5


def items(ks, tab, body):
    def item(t, _):
        n, rho = t >> 2, t & 3
        k = ks[0] if len(ks) == 1 else jnp.where(n == 0, ks[0], ks[1])
        z_keys = (tab[0] + k + NZ) & (NZ - 1)
        both = item_kind(tab, z_keys, 0, rho)[3] & item_kind(tab, z_keys, 1, rho)[3]
        pl.when(both)(lambda: body(n, rho, 0, NK, None, False))

        def one(half, _):
            kind = item_kind(tab, z_keys, half, rho)
            full, some = kind[3:]
            pl.when(full)(lambda: body(n, rho, half, NK // 2, kind, False))
            if 0 in ks or 1 in ks:
                pl.when(jnp.logical_not(full) & some)(lambda: body(n, rho, half, NK // 2, kind, True))
            return 0

        @pl.when(jnp.logical_not(both))
        def _():
            lax.fori_loop(0, 2, one, 0)

        return 0

    lax.fori_loop(0, 4 * len(ks), item, 0)


def stats_body(ks, *refs):
    n_sets = len(ks)
    tab, tag_ref, wide_ref = refs[:3]
    kvs = refs[5 : 5 + n_sets]
    m_ref, l_ref, e_ref, t_ref, kv = refs[5 + n_sets :]
    m_ref[...] = refs[3][...]
    l_ref[...] = refs[4][...]
    take_sets(kv, kvs)

    def body(n, rho, half, size, kind, masked):
        rows = pl.ds(pl.multiple_of(half * 256, 256), size)
        keys = kv[n, rows, 0:HD]
        if masked:
            vis = visible_of(kv, n, half, *kind[:3], tag_ref[rho, :, 0:128])
        for p in range(4):
            cols = slice(256 * p, 256 * p + 256)
            s = dot_nn(keys, wide_ref[rho, :, cols])
            if masked:
                s = jnp.where(vis, s, NEG)
            m_old = m_ref[rho, :, cols]
            m_new = jnp.maximum(m_old, jnp.max(s, axis=0, keepdims=True))
            e = jnp.exp2((s - m_new) * C2)
            if masked:
                e = jnp.where(vis, e, 0.0)
            e_ref[n * 4 + rho, rows, cols] = e.astype(BF16)
            t_ref[(n * 4 + rho) * 2 + half, :, cols] = m_new
            l_ref[rho, :, cols] = l_ref[rho, :, cols] * jnp.exp2((m_old - m_new) * C2) + jnp.sum(
                e, axis=0, keepdims=True
            )
            m_ref[rho, :, cols] = m_new

    items(ks, tab, body)


def grads_body(ks, first, *refs):
    n_sets = len(ks)
    tab, mean_ref, log_ref, qt_ref, gw_ref, gt_ref, e_ref, t_ref = refs[:8]
    kvs, rest = refs[8 : 8 + n_sets], refs[8 + n_sets :]
    dq_ref, acc, kv, p_all, d_all = rest if first else rest[1:]
    if first:

        def wipe(t):
            dq_ref[:, :, lanes(t)] = jnp.zeros((4, HD, 128), F32)

        each(H, wipe)
    take_sets(kv, kvs)

    def clear(t):
        acc[:, lanes(t), :] = jnp.zeros((n_sets, 128, 2 * HD), F32)

    each(NK // 128, clear)

    def body(n, rho, half, size, kind, masked):
        rows = pl.ds(pl.multiple_of(half * 256, 256), size)
        keys = kv[n, rows, 0:HD]
        vals = kv[n, rows, HD:]
        for p in range(4):
            cols = slice(256 * p, 256 * p + 256)
            dp = dot_nn(vals, gw_ref[rho, :, cols])
            share = jnp.exp2((t_ref[(n * 4 + rho) * 2 + half, :, cols] - log_ref[rho, :, cols]) * C2)
            prob = e_ref[n * 4 + rho, rows, cols].astype(F32) * share
            p_all[0:size, cols] = prob.astype(BF16)
            d_all[0:size, cols] = (prob * (dp - mean_ref[rho, :, cols])).astype(BF16)
        d = d_all[0:size, :]
        acc[n, rows, 0:HD] += dot_nn(d, qt_ref[rho])
        acc[n, rows, HD:] += dot_nn(p_all[0:size, :], gt_ref[rho])
        dq_ref[rho] += dot_tn(keys, d)

    items_seen(ks, tab, body)


def items_seen(ks, tab, body):
    def item(t, _):
        n, rho = t >> 2, t & 3
        k = ks[0] if len(ks) == 1 else jnp.where(n == 0, ks[0], ks[1])
        z_keys = (tab[0] + k + NZ) & (NZ - 1)
        both = item_kind(tab, z_keys, 0, rho)[3] & item_kind(tab, z_keys, 1, rho)[3]
        pl.when(both)(lambda: body(n, rho, 0, NK, None, False))

        def one(half, _):
            full, some = item_kind(tab, z_keys, half, rho)[3:]
            pl.when(full | some)(lambda: body(n, rho, half, NK // 2, None, False))
            return 0

        @pl.when(jnp.logical_not(both))
        def _():
            lax.fori_loop(0, 2, one, 0)

        return 0

    lax.fori_loop(0, 4 * len(ks), item, 0)


def emit_body(dq_ref, o0, o1, o2, o3):
    def head(h):
        for rho, out in enumerate((o0, o1, o2, o3)):
            out[:, lanes(h)] = (dq_ref[rho, :, lanes(h)].T * SCALE).astype(BF16)

    each(H, head)


def place_body(tab, a0, a1, a2, a3, q0, q1, q2, gq_ref, gk_ref, gv_ref):
    col = tab[1]
    for rho, part in enumerate((a0, a1, a2, a3)):
        rows = pl.ds(pl.multiple_of((col ^ rho) * 128, 128), 128)
        gk_ref[rows, :] = part[:, 0:HD]
        gv_ref[rows, :] = part[:, HD:]
    total = q0[...].astype(F32) + q1[...].astype(F32) + q2[...].astype(F32)
    gq_ref[...] = total.astype(BF16)


def per_device(queries, keys, values, grad_out, saved_out, segment_ids, frame_flags):
    hop = functools.partial(lax.ppermute, axis_name="ctx")
    rank = lax.axis_index("ctx").astype(jnp.int32)
    tab = jnp.stack([(rank >> 1) & 7, 2 * (rank >> 4) + (rank & 1)])
    hbm = pl.BlockSpec(memory_space=pltpu.HBM)

    *parts, q_own = call(
        begin_body, [shape((144, 256))] * 4 + [shape((NQ + 16, H * HD))], [SM] + [hbm] * 5, nbytes=MIB,
        scratch=[
            pltpu.VMEM((NK, HD), BF16), pltpu.VMEM((NK, HD), BF16), pltpu.VMEM((1, NK), jnp.int32),
            pltpu.VMEM((1, 128), jnp.int32), pltpu.SemaphoreType.DMA((5,)),
        ],
        vmem=58,
    )(tab, keys[0], values[0], segment_ids, frame_flags, queries[0])
    got = [hop(parts[r], perm=flip(r)) for r in (1, 2, 3)]
    own_set = call(join_body, shape((NK + 16, 256)), [VM] * 4, nbytes=MIB)(parts[0], *got)

    def four(x):
        other = hop(x, perm=flip(2))
        return (x, hop(x, perm=flip(1)), other, hop(other, perm=flip(1)))

    q_four = four(q_own)
    g_own = call(cotangent_body, shape((NQ + 16, H * HD)), [VM] * 2, nbytes=MIB)(grad_out[0], saved_out[0])
    forms = [shape((4, NQ * H, HD)), shape((4, HD, NQ * H)), shape((4, 1, NQ * H), F32)]

    def turned(four_of, pieces):
        return call(functools.partial(turn_body, pieces), forms, [VM] * 4, vmem=16, nbytes=4 * MIB)(*four_of)

    q_tall, q_wide, tag = turned(q_four, 1)
    stat = shape((4, 1, NQ * H), F32)
    m = jnp.full((4, 1, NQ * H), NEG, F32)
    l = jnp.zeros((4, 1, NQ * H), F32)
    sets = {0: own_set}
    kept = {}
    fwd = bwd = own_set
    for step in range(5):
        ks = (0,) if step == 0 else (4,) if step == 4 else (step, -step)
        n = len(ks)
        if step < 3:
            fwd, bwd = hop(fwd, perm=turn(1)), hop(bwd, perm=turn(-1))
        elif step == 3:
            bwd = hop(bwd, perm=turn(-1))
        m, l, *kept[ks] = call(
            functools.partial(stats_body, ks),
            [stat, stat, shape((4 * n, NK, NQ * H)), shape((8 * n, 1, NQ * H), F32)],
            [SM] + [VM] * (4 + n), vmem=5,
            scratch=[pltpu.VMEM((n, NK + 16, 256), BF16)], flops=n * (1 << 29), nbytes=2 * MIB,
        )(tab, tag, q_wide, m, l, *[sets[k] for k in ks])
        if step < 4:
            fwd, bwd, m, l = lax.optimization_barrier((fwd, bwd, m, l))
            sets[step + 1] = bwd
            if step < 3:
                sets[-step - 1] = fwd
        if step == 0:
            g_four = four(g_own)
    g_tall, g_wide, mean = turned(g_four, 3)

    ml = jnp.concatenate([m, l], axis=0)
    tops, sums = [m], [l]
    for r in (1, 2, 3):
        got = hop(ml, perm=flip(r))
        tops.append(jnp.concatenate([got[rho ^ r : (rho ^ r) + 1] for rho in range(4)], axis=0))
        sums.append(jnp.concatenate([got[4 + (rho ^ r) : 5 + (rho ^ r)] for rho in range(4)], axis=0))
    top = functools.reduce(jnp.maximum, tops)
    total = sum(s * jnp.exp2((t - top) * C2) for s, t in zip(sums, tops))
    log_total = top + jnp.log2(total) * (1.0 / C2)

    dq = None
    up = down = None
    dq_shape = shape((4, HD, NQ * H), F32)
    for ks in ((4,), (3, -3), (2, -2), (1, -1), (0,)):
        n = len(ks)
        first = dq is None
        args = [tab, mean, log_total, q_tall, g_wide, g_tall, *kept[ks]] + [sets[k] for k in ks]
        args += [] if first else [dq]
        dq, adds = call(
            functools.partial(grads_body, ks, first), [dq_shape, shape((n, NK, 2 * HD), F32)],
            [SM] + [VM] * (len(args) - 1),
            scratch=[pltpu.VMEM((n, NK + 16, 256), BF16)] + [pltpu.VMEM((NK, NQ * H), BF16)] * 2,
            vmem=8, flops=n * 5 * (1 << 29), nbytes=8 * MIB,
            alias={} if first else {len(args) - 1: 0},
        )(*args)
        if ks[0] == 0:
            own = adds[0] + up.astype(F32) + down.astype(F32)
            break
        sends = [(adds[0] if up is None else adds[0] + up.astype(F32)).astype(BF16)]
        if n == 2:
            sends.append((adds[1] if down is None else adds[1] + down.astype(F32)).astype(BF16))
        dq, *sends = lax.optimization_barrier((dq, *sends))
        up = hop(sends[0], perm=turn(1))
        if n == 2:
            down = hop(sends[1], perm=turn(-1))
    scales = jnp.where(jnp.arange(2 * HD) < HD, SCALE, 1.0).astype(F32)
    own = (own * scales[None, :]).astype(BF16)
    dq_four = call(emit_body, [shape((NQ, H * HD))] * 4, [VM], vmem=16, nbytes=3 * MIB)(dq)
    across = dq_four[2].astype(F32) + hop(dq_four[3], perm=flip(1)).astype(F32)
    q_back = [dq_four[0], hop(dq_four[1], perm=flip(1)), hop(across.astype(BF16), perm=flip(2))]
    a_back = [own[0:128]] + [hop(own[128 * r : 128 * r + 128], perm=flip(r)) for r in (1, 2, 3)]
    gq, gk, gv = call(
        place_body, [shape((NQ, H * HD)), shape((NK, HD)), shape((NK, HD))], [SM] + [VM] * 7,
        nbytes=2 * MIB,
    )(tab, *a_back, *q_back)
    return gq[None], gk[None], gv[None]


def solution(mesh):
    row = P("dp", "ctx", None)
    return jax.shard_map(
        per_device,
        mesh=mesh,
        in_specs=(row, row, row, row, row, P("dp", "ctx"), P("dp", None)),
        out_specs=(row, row, row),
        check_vma=False,
    )
```

```python
import functools
import math

import jax
import jax.numpy as jnp
from jax import lax
from jax.experimental import pallas as pl
from jax.experimental.pallas import tpu as pltpu
from jax.sharding import PartitionSpec as P


H = 8
HD = 128
NQ = 128
NK = 512
NZ = 8
SCALE = 1.0 / math.sqrt(HD)
C2 = SCALE * math.log2(math.e)
NEG = -1e30
F32 = jnp.float32
BF16 = jnp.bfloat16
VM = pl.BlockSpec(memory_space=pltpu.VMEM)
SM = pl.BlockSpec(memory_space=pltpu.SMEM)
MIB = 1 << 20


def flip(rho):
    mask = (rho & 1) | ((rho >> 1) << 4)
    return [(i, i ^ mask) for i in range(32)]


def turn(step):
    return [(i, (i // 16) * 16 + (i % 16 + 2 * step) % 16) for i in range(32)]


def dot_nn(left, right):
    return lax.dot_general(left, right, (((1,), (0,)), ((), ())), preferred_element_type=F32)


def dot_tn(left, right):
    return lax.dot_general(left, right, (((0,), (0,)), ((), ())), preferred_element_type=F32)


def call(body, out, specs, scratch=(), vmem=8, flops=0, nbytes=0, alias=None):
    return pl.pallas_call(
        body,
        out_shape=out,
        in_specs=specs,
        out_specs=jax.tree.map(lambda _: VM, out),
        scratch_shapes=list(scratch),
        input_output_aliases=alias or {},
        cost_estimate=pl.CostEstimate(flops=flops, bytes_accessed=nbytes, transcendentals=0),
        compiler_params=pltpu.CompilerParams(vmem_limit_bytes=vmem * MIB),
    )


def shape(dims, dtype=BF16):
    return jax.ShapeDtypeStruct(dims, dtype)


def each(count, body):
    lax.fori_loop(0, count, lambda t, _: (body(t), 0)[1], 0)


def lanes(t):
    return pl.ds(pl.multiple_of(t * 128, 128), 128)


def take_sets(kv, kvs):
    def rows(t):
        part = pl.ds(pl.multiple_of(t * 48, 16), 48)
        for n in range(len(kvs)):
            kv[n, part, :] = kvs[n][part, :]

    each(11, rows)


def column(row):
    return jnp.broadcast_to(row, (128, 128)).T


def begin_body(tab, k_hbm, v_hbm, seg_hbm, flag_hbm, q_hbm, o0, o1, o2, o3, q_out, k_ref, v_ref, seg_ref, flag_ref, sems):
    moves = [
        pltpu.make_async_copy(source, target, sems.at[n])
        for n, (source, target) in enumerate(
            [(seg_hbm, seg_ref), (flag_hbm, flag_ref), (k_hbm, k_ref), (v_hbm, v_ref), (q_hbm, q_out.at[0:NQ, :])]
        )
    ]
    for move in moves:
        move.start()
    moves[0].wait()
    moves[1].wait()
    own = seg_ref[:, NK - NQ :]
    ident = lax.broadcasted_iota(jnp.int32, (128, 128), 0)
    framed = jnp.sum(jnp.where(ident == own, column(flag_ref[...]), 0), axis=0, keepdims=True)
    tag = jnp.where(framed == 1, own, -1).astype(F32)
    q_out[NQ:, :] = jnp.broadcast_to(jnp.concatenate([tag] * H, axis=1), (16, H * HD)).astype(BF16)
    moves[2].wait()
    moves[3].wait()
    for rho, out in enumerate((o0, o1, o2, o3)):
        first = pl.multiple_of((tab[1] ^ rho) * 128, 128)
        out[0:128, 0:HD] = k_ref[pl.ds(first, 128), :]
        out[0:128, HD:] = v_ref[pl.ds(first, 128), :]
        seg = seg_ref[:, pl.ds(first, 128)].astype(F32)
        out[128:, :] = jnp.broadcast_to(jnp.concatenate([seg, seg], axis=1), (16, 256)).astype(BF16)
    moves[4].wait()


def join_body(p0, p1, p2, p3, out):
    row = lax.broadcasted_iota(jnp.int32, (16, 256), 0)
    seg = jnp.zeros((16, 256), F32)
    for rho, part in enumerate((p0, p1, p2, p3)):
        out[128 * rho : 128 * rho + 128, :] = part[0:128, :]
        seg = jnp.where(row == rho, part[128:, :].astype(F32), seg)
    out[NK:, :] = seg.astype(BF16)


def cotangent_body(g_ref, saved_ref, out_ref):
    out_ref[0:NQ, :] = g_ref[...]
    row = lax.broadcasted_iota(jnp.int32, (16, HD), 0)
    for h in range(H):
        cols = slice(h * HD, h * HD + HD)
        both = g_ref[:, cols].astype(F32) * saved_ref[:, cols].astype(F32)
        mean = jnp.sum(both.T, axis=0, keepdims=True)
        top = mean.astype(BF16).astype(F32)
        mid = (mean - top).astype(BF16).astype(F32)
        low = mean - top - mid
        out_ref[NQ:, cols] = jnp.where(row == 0, top, jnp.where(row == 1, mid, low)).astype(BF16)


def turn_body(pieces, q0, q1, q2, q3, tall_ref, wide_ref, row_ref):
    def head(h):
        for rho, q in enumerate((q0, q1, q2, q3)):
            tile = q[0:NQ, lanes(h)]
            tall_ref[rho, lanes(h), :] = tile
            wide_ref[rho, :, lanes(h)] = tile.astype(F32).T.astype(BF16)

    each(H, head)
    for rho, q in enumerate((q0, q1, q2, q3)):
        extra = q[NQ:, :].astype(F32)
        row = extra[0:1, :]
        for n in range(1, pieces):
            row = row + extra[n : n + 1, :]
        row_ref[rho] = row


def item_kind(tab, z_keys, half, rho):
    z, col = tab[0], tab[1]
    own = col ^ rho
    block = 16 * (own >> 1) + 2 * z + (own & 1)
    b0 = col ^ (2 * half)
    b1 = b0 ^ 1
    p0 = (16 * (b0 >> 1) + 2 * z_keys + (b0 & 1)) * NK + 128 * col
    p1 = (16 * (b1 >> 1) + 2 * z_keys + (b1 & 1)) * NK + 128 * col
    first = block * NK + NK - NQ
    full = jnp.maximum(p0, p1) + 127 <= first
    some = jnp.minimum(p0, p1) <= first + NQ - 1 + 1023
    return p0, p1, first, full, some


def visible_of(kv, n, half, p0, p1, first, tag):
    row = lax.broadcasted_iota(jnp.int32, (128, NQ), 0)
    query = lax.broadcasted_iota(jnp.int32, (128, NQ), 1) + first
    seg = kv[n, NK:, 0:128].astype(F32)
    which = lax.broadcasted_iota(jnp.int32, (16, 128), 0)
    parts = []
    for c, p in enumerate((p0, p1)):
        line = jnp.sum(jnp.where(which == 2 * half + c, seg, 0.0), axis=0, keepdims=True)
        parts.append(jnp.where((p + row <= query) | (column(line) == tag), 1.0, 0.0))
    both = jnp.concatenate(parts, axis=0)
    return jnp.concatenate([both, both], axis=1) > 0.5


def items(ks, rhos, tab, body, masks):
    edge = 0 in ks or 1 in ks
    own = ks == (0,)

    def item(t, _):
        n = t // len(rhos)
        rho = rhos[0] + t % len(rhos)
        k = ks[0] if len(ks) == 1 else jnp.where(n == 0, ks[0], ks[1])
        z_keys = (tab[0] + k + NZ) & (NZ - 1)

        def one(half, _):
            kind = item_kind(tab, z_keys, half, rho)
            full, some = kind[3:]
            if edge:
                pl.when(full | some)(lambda: body(n, rho, half, NK // 2, kind, masks))
            else:
                pl.when(full)(lambda: body(n, rho, half, NK // 2, kind, False))
            return 0

        if own:
            lax.fori_loop(0, 2, one, 0)
        else:
            both = item_kind(tab, z_keys, 0, rho)[3] & item_kind(tab, z_keys, 1, rho)[3]
            pl.when(both)(lambda: body(n, rho, 0, NK, None, False))

            @pl.when(jnp.logical_not(both))
            def _():
                lax.fori_loop(0, 2, one, 0)

        return 0

    lax.fori_loop(0, len(rhos) * len(ks), item, 0)


def stats_body(ks, *refs):
    n_sets = len(ks)
    tab, tag_ref, wide_ref = refs[:3]
    kvs = refs[5 : 5 + n_sets]
    m_ref, l_ref, e_ref, t_ref, kv = refs[5 + n_sets :]
    m_ref[...] = refs[3][...]
    l_ref[...] = refs[4][...]
    take_sets(kv, kvs)

    def body(n, rho, half, size, kind, masked):
        rows = pl.ds(pl.multiple_of(half * 256, 256), size)
        keys = kv[n, rows, 0:HD]
        if masked:
            vis = visible_of(kv, n, half, *kind[:3], tag_ref[rho, :, 0:128])
        for p in range(4):
            cols = slice(256 * p, 256 * p + 256)
            s = dot_nn(keys, wide_ref[rho, :, cols])
            if masked:
                s = jnp.where(vis, s, NEG)
            m_old = m_ref[rho, :, cols]
            m_new = jnp.maximum(m_old, jnp.max(s, axis=0, keepdims=True))
            e = jnp.exp2((s - m_new) * C2)
            if masked:
                e = jnp.where(vis, e, 0.0)
            e_ref[n * 4 + rho, rows, cols] = e.astype(BF16)
            t_ref[(n * 4 + rho) * 2 + half, :, cols] = m_new
            l_ref[rho, :, cols] = l_ref[rho, :, cols] * jnp.exp2((m_old - m_new) * C2) + jnp.sum(
                e, axis=0, keepdims=True
            )
            m_ref[rho, :, cols] = m_new

    items(ks, (0, 1, 2, 3), tab, body, True)


def grads_body(ks, rhos, first, last, *refs):
    n_sets = len(ks)
    tab, mean_ref, log_ref, qt_ref, gw_ref, gt_ref, e_ref, t_ref = refs[:8]
    kvs, rest = refs[8 : 8 + n_sets], refs[8 + n_sets :]
    if first:
        dq_ref, acc, kv, p_all, d_all = rest

        def wipe(t):
            dq_ref[:, :, lanes(t)] = jnp.zeros((4, HD, 128), F32)

        each(H, wipe)
    elif last:
        dq_in, o0, o1, acc, kv, p_all, d_all, dq_ref = rest

        def fetch(t):
            dq_ref[:, :, lanes(t)] = dq_in[rhos[0] : rhos[0] + 2, :, lanes(t)]

        each(H, fetch)
    else:
        _, dq_ref, acc, kv, p_all, d_all = rest
    take_sets(kv, kvs)

    def clear(t):
        acc[:, lanes(t), :] = jnp.zeros((n_sets, 128, 2 * HD), F32)

    each(NK // 128, clear)

    def body(n, rho, half, size, kind, masked):
        rows = pl.ds(pl.multiple_of(half * 256, 256), size)
        keys = kv[n, rows, 0:HD]
        vals = kv[n, rows, HD:]
        for p in range(4):
            cols = slice(256 * p, 256 * p + 256)
            dp = dot_nn(vals, gw_ref[rho, :, cols])
            share = jnp.exp2((t_ref[(n * 4 + rho) * 2 + half, :, cols] - log_ref[rho, :, cols]) * C2)
            prob = e_ref[n * 4 + rho, rows, cols].astype(F32) * share
            p_all[0:size, cols] = prob.astype(BF16)
            d_all[0:size, cols] = (prob * (dp - mean_ref[rho, :, cols])).astype(BF16)
        d = d_all[0:size, :]
        acc[n, rows, 0:HD] += dot_nn(d, qt_ref[rho])
        acc[n, rows, HD:] += dot_nn(p_all[0:size, :], gt_ref[rho])
        dq_ref[rho - rhos[0]] += dot_tn(keys, d)

    items(ks, rhos, tab, body, False)
    if last:

        def head(h):
            for r, out in enumerate((o0, o1)):
                out[:, lanes(h)] = (dq_ref[r, :, lanes(h)].T * SCALE).astype(BF16)

        each(H, head)


def place_body(tab, a0, a1, a2, a3, q0, q1, q2, gq_ref, gk_ref, gv_ref):
    col = tab[1]
    for rho, part in enumerate((a0, a1, a2, a3)):
        rows = pl.ds(pl.multiple_of((col ^ rho) * 128, 128), 128)
        gk_ref[rows, :] = part[:, 0:HD]
        gv_ref[rows, :] = part[:, HD:]
    total = q0[...].astype(F32) + q1[...].astype(F32) + q2[...].astype(F32)
    gq_ref[...] = total.astype(BF16)


def per_device(queries, keys, values, grad_out, saved_out, segment_ids, frame_flags):
    hop = functools.partial(lax.ppermute, axis_name="ctx")
    rank = lax.axis_index("ctx").astype(jnp.int32)
    tab = jnp.stack([(rank >> 1) & 7, 2 * (rank >> 4) + (rank & 1)])
    hbm = pl.BlockSpec(memory_space=pltpu.HBM)

    *parts, q_own = call(
        begin_body, [shape((144, 256))] * 4 + [shape((NQ + 16, H * HD))], [SM] + [hbm] * 5, nbytes=MIB,
        scratch=[
            pltpu.VMEM((NK, HD), BF16), pltpu.VMEM((NK, HD), BF16), pltpu.VMEM((1, NK), jnp.int32),
            pltpu.VMEM((1, 128), jnp.int32), pltpu.SemaphoreType.DMA((5,)),
        ],
        vmem=58,
    )(tab, keys[0], values[0], segment_ids, frame_flags, queries[0])
    got = [hop(parts[r], perm=flip(r)) for r in (1, 2, 3)]
    own_set = call(join_body, shape((NK + 16, 256)), [VM] * 4, nbytes=MIB)(parts[0], *got)

    def four(x):
        other = hop(x, perm=flip(2))
        return (x, hop(x, perm=flip(1)), other, hop(other, perm=flip(1)))

    q_four = four(q_own)
    g_own = call(cotangent_body, shape((NQ + 16, H * HD)), [VM] * 2, nbytes=MIB)(grad_out[0], saved_out[0])
    forms = [shape((4, NQ * H, HD)), shape((4, HD, NQ * H)), shape((4, 1, NQ * H), F32)]

    def turned(four_of, pieces):
        return call(functools.partial(turn_body, pieces), forms, [VM] * 4, vmem=16, nbytes=4 * MIB)(*four_of)

    q_tall, q_wide, tag = turned(q_four, 1)
    stat = shape((4, 1, NQ * H), F32)
    m = jnp.full((4, 1, NQ * H), NEG, F32)
    l = jnp.zeros((4, 1, NQ * H), F32)
    sets = {0: own_set}
    kept = {}
    fwd = bwd = own_set
    for step in range(5):
        ks = (0,) if step == 0 else (4,) if step == 4 else (step, -step)
        n = len(ks)
        if step < 3:
            fwd, bwd = hop(fwd, perm=turn(1)), hop(bwd, perm=turn(-1))
        elif step == 3:
            bwd = hop(bwd, perm=turn(-1))
        m, l, *kept[ks] = call(
            functools.partial(stats_body, ks),
            [stat, stat, shape((4 * n, NK, NQ * H)), shape((8 * n, 1, NQ * H), F32)],
            [SM] + [VM] * (4 + n), vmem=3,
            scratch=[pltpu.VMEM((n, NK + 16, 256), BF16)], flops=n * (1 << 29), nbytes=2 * MIB,
        )(tab, tag, q_wide, m, l, *[sets[k] for k in ks])
        if step < 4:
            fwd, bwd, m, l = lax.optimization_barrier((fwd, bwd, m, l))
            sets[step + 1] = bwd
            if step < 3:
                sets[-step - 1] = fwd
        if step == 0:
            g_four = four(g_own)
    g_tall, g_wide, mean = turned(g_four, 3)

    ml = jnp.concatenate([m, l], axis=0)
    tops, sums = [m], [l]
    for r in (1, 2, 3):
        got = hop(ml, perm=flip(r))
        tops.append(jnp.concatenate([got[rho ^ r : (rho ^ r) + 1] for rho in range(4)], axis=0))
        sums.append(jnp.concatenate([got[4 + (rho ^ r) : 5 + (rho ^ r)] for rho in range(4)], axis=0))
    top = functools.reduce(jnp.maximum, tops)
    total = sum(s * jnp.exp2((t - top) * C2) for s, t in zip(sums, tops))
    log_total = top + jnp.log2(total) * (1.0 / C2)

    dq = None
    up = down = None
    dq_shape = shape((4, HD, NQ * H), F32)

    def grads(ks, rhos, dq):
        n = len(ks)
        first, last = dq is None, ks == (0,)
        args = [tab, mean, log_total, q_tall, g_wide, g_tall, *kept[ks]] + [sets[k] for k in ks]
        args += [] if first else [dq]
        piece = shape((NQ, H * HD))
        scratch = [pltpu.VMEM((n, NK + 16, 256), BF16)] + [pltpu.VMEM((NK, NQ * H), BF16)] * 2
        return call(
            functools.partial(grads_body, ks, rhos, first, last),
            ([piece, piece] if last else [dq_shape]) + [shape((n, NK, 2 * HD), F32)],
            [SM] + [VM] * (len(args) - 1),
            scratch=scratch + ([pltpu.VMEM((2, HD, NQ * H), F32)] if last else []),
            vmem=5, flops=n * 5 * (1 << 29), nbytes=8 * MIB,
            alias={} if first or last else {len(args) - 1: 0},
        )(*args)

    for ks in ((4,), (3, -3), (2, -2), (1, -1)):
        n = len(ks)
        dq, adds = grads(ks, (0, 1, 2, 3), dq)
        sends = [(adds[0] if up is None else adds[0] + up.astype(F32)).astype(BF16)]
        if n == 2:
            sends.append((adds[1] if down is None else adds[1] + down.astype(F32)).astype(BF16))
        dq, *sends = lax.optimization_barrier((dq, *sends))
        up = hop(sends[0], perm=turn(1))
        if n == 2:
            down = hop(sends[1], perm=turn(-1))
    dq2, dq3, far_adds = grads((0,), (2, 3), dq)
    dq3 = hop(dq3, perm=flip(1))
    across = (dq2.astype(F32) + dq3.astype(F32)).astype(BF16)
    dq_far = hop(across, perm=flip(2))
    dq0, dq1, near_adds = grads((0,), (0, 1), dq)
    own = far_adds[0] + near_adds[0] + up.astype(F32) + down.astype(F32)
    scales = jnp.where(jnp.arange(2 * HD) < HD, SCALE, 1.0).astype(F32)
    own = (own * scales[None, :]).astype(BF16)
    q_back = [dq0, hop(dq1, perm=flip(1)), dq_far]
    a_back = [own[0:128]] + [hop(own[128 * r : 128 * r + 128], perm=flip(r)) for r in (1, 2, 3)]
    gq, gk, gv = call(
        place_body, [shape((NQ, H * HD)), shape((NK, HD)), shape((NK, HD))], [SM] + [VM] * 7,
        nbytes=2 * MIB,
    )(tab, *a_back, *q_back)
    return gq[None], gk[None], gv[None]


def solution(mesh):
    row = P("dp", "ctx", None)
    return jax.shard_map(
        per_device,
        mesh=mesh,
        in_specs=(row, row, row, row, row, P("dp", "ctx"), P("dp", None)),
        out_specs=(row, row, row),
        check_vma=False,
    )
```

```python
import functools
import math

import jax
import jax.numpy as jnp
from jax import lax
from jax.experimental import pallas as pl
from jax.experimental.pallas import tpu as pltpu
from jax.sharding import PartitionSpec as P


H = 8
HD = 128
NQ = 128
NK = 512
NZ = 8
SCALE = 1.0 / math.sqrt(HD)
C2 = SCALE * math.log2(math.e)
NEG = -1e30
F32 = jnp.float32
BF16 = jnp.bfloat16
VM = pl.BlockSpec(memory_space=pltpu.VMEM)
SM = pl.BlockSpec(memory_space=pltpu.SMEM)
MIB = 1 << 20


def flip(rho):
    mask = (rho & 1) | ((rho >> 1) << 4)
    return [(i, i ^ mask) for i in range(32)]


def turn(step):
    return [(i, (i // 16) * 16 + (i % 16 + 2 * step) % 16) for i in range(32)]


def dot_nn(left, right):
    return lax.dot_general(left, right, (((1,), (0,)), ((), ())), preferred_element_type=F32)


def dot_tn(left, right):
    return lax.dot_general(left, right, (((0,), (0,)), ((), ())), preferred_element_type=F32)


def call(body, out, specs, scratch=(), vmem=8, flops=0, nbytes=0, alias=None):
    return pl.pallas_call(
        body,
        out_shape=out,
        in_specs=specs,
        out_specs=jax.tree.map(lambda _: VM, out),
        scratch_shapes=list(scratch),
        input_output_aliases=alias or {},
        cost_estimate=pl.CostEstimate(flops=flops, bytes_accessed=nbytes, transcendentals=0),
        compiler_params=pltpu.CompilerParams(vmem_limit_bytes=vmem * MIB),
    )


def shape(dims, dtype=BF16):
    return jax.ShapeDtypeStruct(dims, dtype)


def each(count, body):
    lax.fori_loop(0, count, lambda t, _: (body(t), 0)[1], 0)


def lanes(t):
    return pl.ds(pl.multiple_of(t * 128, 128), 128)


def take_sets(kv, kvs):
    def rows(t):
        part = pl.ds(pl.multiple_of(t * 48, 16), 48)
        for n in range(len(kvs)):
            kv[n, part, :] = kvs[n][part, :]

    each(11, rows)


def column(row):
    return jnp.broadcast_to(row, (128, 128)).T


def begin_body(tab, k_hbm, v_hbm, seg_hbm, flag_hbm, q_hbm, o0, o1, o2, o3, q_out, k_ref, v_ref, seg_ref, flag_ref, sems):
    moves = [
        pltpu.make_async_copy(source, target, sems.at[n])
        for n, (source, target) in enumerate(
            [(seg_hbm, seg_ref), (flag_hbm, flag_ref), (k_hbm, k_ref), (v_hbm, v_ref), (q_hbm, q_out.at[0:NQ, :])]
        )
    ]
    for move in moves:
        move.start()
    moves[0].wait()
    moves[1].wait()
    own = seg_ref[:, NK - NQ :]
    ident = lax.broadcasted_iota(jnp.int32, (128, 128), 0)
    framed = jnp.sum(jnp.where(ident == own, column(flag_ref[...]), 0), axis=0, keepdims=True)
    tag = jnp.where(framed == 1, own, -1).astype(F32)
    q_out[NQ:, :] = jnp.broadcast_to(jnp.concatenate([tag] * H, axis=1), (16, H * HD)).astype(BF16)
    moves[2].wait()
    moves[3].wait()
    for rho, out in enumerate((o0, o1, o2, o3)):
        first = pl.multiple_of((tab[1] ^ rho) * 128, 128)
        out[0:128, 0:HD] = k_ref[pl.ds(first, 128), :]
        out[0:128, HD:] = v_ref[pl.ds(first, 128), :]
        seg = seg_ref[:, pl.ds(first, 128)].astype(F32)
        out[128:, :] = jnp.broadcast_to(jnp.concatenate([seg, seg], axis=1), (16, 256)).astype(BF16)
    moves[4].wait()


def join_body(p0, p1, p2, p3, out):
    row = lax.broadcasted_iota(jnp.int32, (16, 256), 0)
    seg = jnp.zeros((16, 256), F32)
    for rho, part in enumerate((p0, p1, p2, p3)):
        out[128 * rho : 128 * rho + 128, :] = part[0:128, :]
        seg = jnp.where(row == rho, part[128:, :].astype(F32), seg)
    out[NK:, :] = seg.astype(BF16)


def cotangent_body(g_ref, saved_ref, out_ref):
    out_ref[0:NQ, :] = g_ref[...]
    row = lax.broadcasted_iota(jnp.int32, (16, HD), 0)
    for h in range(H):
        cols = slice(h * HD, h * HD + HD)
        both = g_ref[:, cols].astype(F32) * saved_ref[:, cols].astype(F32)
        mean = jnp.sum(both.T, axis=0, keepdims=True)
        top = mean.astype(BF16).astype(F32)
        mid = (mean - top).astype(BF16).astype(F32)
        low = mean - top - mid
        out_ref[NQ:, cols] = jnp.where(row == 0, top, jnp.where(row == 1, mid, low)).astype(BF16)


def turn_body(pieces, q0, q1, q2, q3, tall_ref, wide_ref, row_ref):
    def head(h):
        for rho, q in enumerate((q0, q1, q2, q3)):
            tile = q[0:NQ, lanes(h)]
            tall_ref[rho, lanes(h), :] = tile
            wide_ref[rho, :, lanes(h)] = tile.astype(F32).T.astype(BF16)

    each(H, head)
    for rho, q in enumerate((q0, q1, q2, q3)):
        extra = q[NQ:, :].astype(F32)
        row = extra[0:1, :]
        for n in range(1, pieces):
            row = row + extra[n : n + 1, :]
        row_ref[rho] = row


def item_kind(tab, z_keys, half, rho):
    z, col = tab[0], tab[1]
    own = col ^ rho
    block = 16 * (own >> 1) + 2 * z + (own & 1)
    b0 = col ^ (2 * half)
    b1 = b0 ^ 1
    p0 = (16 * (b0 >> 1) + 2 * z_keys + (b0 & 1)) * NK + 128 * col
    p1 = (16 * (b1 >> 1) + 2 * z_keys + (b1 & 1)) * NK + 128 * col
    first = block * NK + NK - NQ
    full = jnp.maximum(p0, p1) + 127 <= first
    some = jnp.minimum(p0, p1) <= first + NQ - 1 + 1023
    return p0, p1, first, full, some


def visible_of(kv, n, half, p0, p1, first, tag):
    row = lax.broadcasted_iota(jnp.int32, (128, NQ), 0)
    query = lax.broadcasted_iota(jnp.int32, (128, NQ), 1) + first
    seg = kv[n, NK:, 0:128].astype(F32)
    which = lax.broadcasted_iota(jnp.int32, (16, 128), 0)
    parts = []
    for c, p in enumerate((p0, p1)):
        line = jnp.sum(jnp.where(which == 2 * half + c, seg, 0.0), axis=0, keepdims=True)
        parts.append(jnp.where((p + row <= query) | (column(line) == tag), 1.0, 0.0))
    both = jnp.concatenate(parts, axis=0)
    return jnp.concatenate([both, both], axis=1) > 0.5


def items(ks, rhos, tab, body, masks):
    edge = 0 in ks or 1 in ks
    own = ks == (0,)

    def item(t, _):
        n = t // len(rhos)
        rho = rhos[0] + t % len(rhos)
        k = ks[0] if len(ks) == 1 else jnp.where(n == 0, ks[0], ks[1])
        z_keys = (tab[0] + k + NZ) & (NZ - 1)

        def one(half, _):
            kind = item_kind(tab, z_keys, half, rho)
            full, some = kind[3:]
            if edge:
                pl.when(full | some)(lambda: body(n, rho, half, NK // 2, kind, masks))
            else:
                pl.when(full)(lambda: body(n, rho, half, NK // 2, kind, False))
            return 0

        if own:
            lax.fori_loop(0, 2, one, 0)
        else:
            both = item_kind(tab, z_keys, 0, rho)[3] & item_kind(tab, z_keys, 1, rho)[3]
            pl.when(both)(lambda: body(n, rho, 0, NK, None, False))

            @pl.when(jnp.logical_not(both))
            def _():
                lax.fori_loop(0, 2, one, 0)

        return 0

    lax.fori_loop(0, len(rhos) * len(ks), item, 0)


def stats_body(ks, *refs):
    n_sets = len(ks)
    tab, tag_ref, wide_ref = refs[:3]
    kvs = refs[5 : 5 + n_sets]
    m_ref, l_ref, e_ref, t_ref, kv, sum_ref, top_ref = refs[5 + n_sets :]
    m_ref[...] = refs[3][...]
    l_ref[...] = refs[4][...]
    take_sets(kv, kvs)

    def inputs(n, rho, half, size, kind, masked):
        rows = pl.ds(pl.multiple_of(half * 256, 256), size)
        vis = visible_of(kv, n, half, *kind[:3], tag_ref[rho, :, 0:128]) if masked else None
        return rows, kv[n, rows, 0:HD], vis

    def scores(keys, rho, cols, vis):
        s = dot_nn(keys, wide_ref[rho, :, cols])
        return s if vis is None else jnp.where(vis, s, NEG)

    def first_body(n, rho, half, size, kind, masked):
        rows, keys, vis = inputs(n, rho, half, size, kind, masked)
        for p in range(4):
            cols = slice(256 * p, 256 * p + 256)
            s = scores(keys, rho, cols, vis)
            m_old = m_ref[rho, :, cols]
            m_new = jnp.maximum(m_old, jnp.max(s, axis=0, keepdims=True))
            e = jnp.exp2((s - m_new) * C2)
            if masked:
                e = jnp.where(vis, e, 0.0)
            e_ref[n * 4 + rho, rows, cols] = e.astype(BF16)
            t_ref[(n * 4 + rho) * 2 + half, :, cols] = m_new
            l_ref[rho, :, cols] = l_ref[rho, :, cols] * jnp.exp2((m_old - m_new) * C2) + jnp.sum(
                e, axis=0, keepdims=True
            )
            m_ref[rho, :, cols] = m_new

    def later_body(n, rho, half, size, kind, masked):
        rows, keys, vis = inputs(n, rho, half, size, kind, masked)
        slot = (n * 4 + rho) * 2 + half
        t_ref[slot] = m_ref[rho]
        top_ref[...] = m_ref[rho]

        def attempt(_):
            ref = jnp.maximum(t_ref[slot], top_ref[...])
            t_ref[slot] = ref
            for p in range(4):
                cols = slice(256 * p, 256 * p + 256)
                s = scores(keys, rho, cols, vis)
                e = jnp.exp2((s - t_ref[slot, :, cols]) * C2)
                e_ref[n * 4 + rho, rows, cols] = e.astype(BF16)
                sum_ref[:, cols] = jnp.sum(e, axis=0, keepdims=True)
                top_ref[:, cols] = jnp.max(s, axis=0, keepdims=True)
            return jnp.max((top_ref[...] - ref) * C2)

        lax.while_loop(lambda over: over > 32.0, attempt, jnp.float32(64.0))
        ref = t_ref[slot]
        l_ref[rho] = l_ref[rho] * jnp.exp2((m_ref[rho] - ref) * C2) + sum_ref[...]
        m_ref[rho] = ref

    items(ks, (0, 1, 2, 3), tab, first_body if ks == (0,) else later_body, True)


def grads_body(ks, rhos, first, last, *refs):
    n_sets = len(ks)
    tab, mean_ref, log_ref, qt_ref, gw_ref, gt_ref, e_ref, t_ref = refs[:8]
    kvs, rest = refs[8 : 8 + n_sets], refs[8 + n_sets :]
    if first:
        dq_ref, acc, kv, p_all, d_all = rest

        def wipe(t):
            dq_ref[:, :, lanes(t)] = jnp.zeros((4, HD, 128), F32)

        each(H, wipe)
    elif last:
        dq_in, o0, o1, acc, kv, p_all, d_all, dq_ref = rest

        def fetch(t):
            dq_ref[:, :, lanes(t)] = dq_in[rhos[0] : rhos[0] + 2, :, lanes(t)]

        each(H, fetch)
    else:
        _, dq_ref, acc, kv, p_all, d_all = rest
    take_sets(kv, kvs)

    def clear(t):
        acc[:, lanes(t), :] = jnp.zeros((n_sets, 128, 2 * HD), F32)

    each(NK // 128, clear)

    def body(n, rho, half, size, kind, masked):
        rows = pl.ds(pl.multiple_of(half * 256, 256), size)
        keys = kv[n, rows, 0:HD]
        vals = kv[n, rows, HD:]
        for p in range(4):
            cols = slice(256 * p, 256 * p + 256)
            dp = dot_nn(vals, gw_ref[rho, :, cols])
            share = jnp.exp2((t_ref[(n * 4 + rho) * 2 + half, :, cols] - log_ref[rho, :, cols]) * C2)
            prob = e_ref[n * 4 + rho, rows, cols].astype(F32) * share
            p_all[0:size, cols] = prob.astype(BF16)
            d_all[0:size, cols] = (prob * (dp - mean_ref[rho, :, cols])).astype(BF16)
        d = d_all[0:size, :]
        acc[n, rows, 0:HD] += dot_nn(d, qt_ref[rho])
        acc[n, rows, HD:] += dot_nn(p_all[0:size, :], gt_ref[rho])
        dq_ref[rho - rhos[0]] += dot_tn(keys, d)

    items(ks, rhos, tab, body, False)
    if last:

        def head(h):
            for r, out in enumerate((o0, o1)):
                out[:, lanes(h)] = (dq_ref[r, :, lanes(h)].T * SCALE).astype(BF16)

        each(H, head)


def place_body(tab, a0, a1, a2, a3, q0, q1, q2, gq_ref, gk_ref, gv_ref):
    col = tab[1]
    for rho, part in enumerate((a0, a1, a2, a3)):
        rows = pl.ds(pl.multiple_of((col ^ rho) * 128, 128), 128)
        gk_ref[rows, :] = part[:, 0:HD]
        gv_ref[rows, :] = part[:, HD:]
    total = q0[...].astype(F32) + q1[...].astype(F32) + q2[...].astype(F32)
    gq_ref[...] = total.astype(BF16)


def per_device(queries, keys, values, grad_out, saved_out, segment_ids, frame_flags):
    hop = functools.partial(lax.ppermute, axis_name="ctx")
    rank = lax.axis_index("ctx").astype(jnp.int32)
    tab = jnp.stack([(rank >> 1) & 7, 2 * (rank >> 4) + (rank & 1)])
    hbm = pl.BlockSpec(memory_space=pltpu.HBM)

    *parts, q_own = call(
        begin_body, [shape((144, 256))] * 4 + [shape((NQ + 16, H * HD))], [SM] + [hbm] * 5, nbytes=MIB,
        scratch=[
            pltpu.VMEM((NK, HD), BF16), pltpu.VMEM((NK, HD), BF16), pltpu.VMEM((1, NK), jnp.int32),
            pltpu.VMEM((1, 128), jnp.int32), pltpu.SemaphoreType.DMA((5,)),
        ],
        vmem=58,
    )(tab, keys[0], values[0], segment_ids, frame_flags, queries[0])
    got = [hop(parts[r], perm=flip(r)) for r in (1, 2, 3)]
    own_set = call(join_body, shape((NK + 16, 256)), [VM] * 4, nbytes=MIB)(parts[0], *got)

    def four(x):
        other = hop(x, perm=flip(2))
        last = hop(other, perm=flip(1))
        return (x, hop(x, perm=flip(1)), other, last)

    q_four = four(q_own)
    g_own = call(cotangent_body, shape((NQ + 16, H * HD)), [VM] * 2, nbytes=MIB)(grad_out[0], saved_out[0])
    forms = [shape((4, NQ * H, HD)), shape((4, HD, NQ * H)), shape((4, 1, NQ * H), F32)]

    def turned(four_of, pieces):
        return call(functools.partial(turn_body, pieces), forms, [VM] * 4, vmem=16, nbytes=4 * MIB)(*four_of)

    q_tall, q_wide, tag = turned(q_four, 1)
    stat = shape((4, 1, NQ * H), F32)
    m = jnp.full((4, 1, NQ * H), NEG, F32)
    l = jnp.zeros((4, 1, NQ * H), F32)
    sets = {0: own_set}
    kept = {}
    fwd = bwd = own_set
    for step in range(5):
        ks = (0,) if step == 0 else (4,) if step == 4 else (step, -step)
        n = len(ks)
        if step < 3:
            fwd, bwd = hop(fwd, perm=turn(1)), hop(bwd, perm=turn(-1))
        elif step == 3:
            bwd = hop(bwd, perm=turn(-1))
        m, l, *kept[ks] = call(
            functools.partial(stats_body, ks),
            [stat, stat, shape((4 * n, NK, NQ * H)), shape((8 * n, 1, NQ * H), F32)],
            [SM] + [VM] * (4 + n), vmem=3,
            scratch=[pltpu.VMEM((n, NK + 16, 256), BF16)] + [pltpu.VMEM((1, NQ * H), F32)] * 2,
            flops=n * (1 << 29), nbytes=2 * MIB,
        )(tab, tag, q_wide, m, l, *[sets[k] for k in ks])
        if step < 4:
            if step > 0:
                fwd, bwd, m, l = lax.optimization_barrier((fwd, bwd, m, l))
            sets[step + 1] = bwd
            if step < 3:
                sets[-step - 1] = fwd
        if step == 0:
            g_four = four(g_own)
    g_tall, g_wide, mean = turned(g_four, 3)

    ml = jnp.concatenate([m, l], axis=0)
    tops, sums = [m], [l]
    for r in (1, 2, 3):
        got = hop(ml, perm=flip(r))
        tops.append(jnp.concatenate([got[rho ^ r : (rho ^ r) + 1] for rho in range(4)], axis=0))
        sums.append(jnp.concatenate([got[4 + (rho ^ r) : 5 + (rho ^ r)] for rho in range(4)], axis=0))
    top = functools.reduce(jnp.maximum, tops)
    total = sum(s * jnp.exp2((t - top) * C2) for s, t in zip(sums, tops))
    log_total = top + jnp.log2(total) * (1.0 / C2)

    dq = None
    up = down = None
    dq_shape = shape((4, HD, NQ * H), F32)

    def grads(ks, rhos, dq):
        n = len(ks)
        first, last = dq is None, ks == (0,)
        args = [tab, mean, log_total, q_tall, g_wide, g_tall, *kept[ks]] + [sets[k] for k in ks]
        args += [] if first else [dq]
        piece = shape((NQ, H * HD))
        scratch = [pltpu.VMEM((n, NK + 16, 256), BF16)] + [pltpu.VMEM((NK, NQ * H), BF16)] * 2
        return call(
            functools.partial(grads_body, ks, rhos, first, last),
            ([piece, piece] if last else [dq_shape]) + [shape((n, NK, 2 * HD), F32)],
            [SM] + [VM] * (len(args) - 1),
            scratch=scratch + ([pltpu.VMEM((2, HD, NQ * H), F32)] if last else []),
            vmem=5, flops=n * 5 * (1 << 29), nbytes=8 * MIB,
            alias={} if first or last else {len(args) - 1: 0},
        )(*args)

    for ks in ((4,), (3, -3), (2, -2), (1, -1)):
        n = len(ks)
        dq, adds = grads(ks, (0, 1, 2, 3), dq)
        sends = [(adds[0] if up is None else adds[0] + up.astype(F32)).astype(BF16)]
        if n == 2:
            sends.append((adds[1] if down is None else adds[1] + down.astype(F32)).astype(BF16))
        dq, *sends = lax.optimization_barrier((dq, *sends))
        up = hop(sends[0], perm=turn(1))
        if n == 2:
            down = hop(sends[1], perm=turn(-1))
    dq2, dq3, far_adds = grads((0,), (2, 3), dq)
    dq3 = hop(dq3, perm=flip(1))
    across = (dq2.astype(F32) + dq3.astype(F32)).astype(BF16)
    dq_far = hop(across, perm=flip(2))
    dq0, dq1, near_adds = grads((0,), (0, 1), dq)
    own = far_adds[0] + near_adds[0] + up.astype(F32) + down.astype(F32)
    scales = jnp.where(jnp.arange(2 * HD) < HD, SCALE, 1.0).astype(F32)
    own = (own * scales[None, :]).astype(BF16)
    q_back = [dq0, hop(dq1, perm=flip(1)), dq_far]
    a_back = [own[0:128]] + [hop(own[128 * r : 128 * r + 128], perm=flip(r)) for r in (1, 2, 3)]
    gq, gk, gv = call(
        place_body, [shape((NQ, H * HD)), shape((NK, HD)), shape((NK, HD))], [SM] + [VM] * 7,
        nbytes=2 * MIB,
    )(tab, *a_back, *q_back)
    return gq[None], gk[None], gv[None]


def solution(mesh):
    row = P("dp", "ctx", None)
    return jax.shard_map(
        per_device,
        mesh=mesh,
        in_specs=(row, row, row, row, row, P("dp", "ctx"), P("dp", None)),
        out_specs=(row, row, row),
        check_vma=False,
    )
```

```python
import functools
import math

import jax
import jax.numpy as jnp
from jax import lax
from jax.experimental import pallas as pl
from jax.experimental.pallas import tpu as pltpu
from jax.sharding import PartitionSpec as P


H = 8
HD = 128
NQ = 128
NK = 512
NZ = 8
SCALE = 1.0 / math.sqrt(HD)
C2 = SCALE * math.log2(math.e)
NEG = -1e30
F32 = jnp.float32
BF16 = jnp.bfloat16
VM = pl.BlockSpec(memory_space=pltpu.VMEM)
SM = pl.BlockSpec(memory_space=pltpu.SMEM)
MIB = 1 << 20


def flip(rho):
    mask = (rho & 1) | ((rho >> 1) << 4)
    return [(i, i ^ mask) for i in range(32)]


def turn(step):
    return [(i, (i // 16) * 16 + (i % 16 + 2 * step) % 16) for i in range(32)]


def dot_nn(left, right):
    return lax.dot_general(left, right, (((1,), (0,)), ((), ())), preferred_element_type=F32)


def dot_tn(left, right):
    return lax.dot_general(left, right, (((0,), (0,)), ((), ())), preferred_element_type=F32)


def call(body, out, specs, scratch=(), vmem=8, flops=0, nbytes=0, alias=None):
    return pl.pallas_call(
        body,
        out_shape=out,
        in_specs=specs,
        out_specs=jax.tree.map(lambda _: VM, out),
        scratch_shapes=list(scratch),
        input_output_aliases=alias or {},
        cost_estimate=pl.CostEstimate(flops=flops, bytes_accessed=nbytes, transcendentals=0),
        compiler_params=pltpu.CompilerParams(vmem_limit_bytes=vmem * MIB),
    )


def shape(dims, dtype=BF16):
    return jax.ShapeDtypeStruct(dims, dtype)


def each(count, body):
    lax.fori_loop(0, count, lambda t, _: (body(t), 0)[1], 0)


def lanes(t):
    return pl.ds(pl.multiple_of(t * 128, 128), 128)


def take_sets(kv, kvs):
    def rows(t):
        part = pl.ds(pl.multiple_of(t * 48, 16), 48)
        for n in range(len(kvs)):
            kv[n, part, :] = kvs[n][part, :]

    each(11, rows)


def column(row):
    return jnp.broadcast_to(row, (128, 128)).T


def begin_body(tab, k_hbm, v_hbm, seg_hbm, flag_hbm, q_hbm, o0, o1, o2, o3, q_out, k_ref, v_ref, seg_ref, flag_ref, sems):
    moves = [
        pltpu.make_async_copy(source, target, sems.at[n])
        for n, (source, target) in enumerate(
            [(seg_hbm, seg_ref), (flag_hbm, flag_ref), (k_hbm, k_ref), (v_hbm, v_ref), (q_hbm, q_out.at[0:NQ, :])]
        )
    ]
    for move in moves:
        move.start()
    moves[0].wait()
    moves[1].wait()
    own = seg_ref[:, NK - NQ :]
    ident = lax.broadcasted_iota(jnp.int32, (128, 128), 0)
    framed = jnp.sum(jnp.where(ident == own, column(flag_ref[...]), 0), axis=0, keepdims=True)
    tag = jnp.where(framed == 1, own, -1).astype(F32)
    q_out[NQ:, :] = jnp.broadcast_to(jnp.concatenate([tag] * H, axis=1), (16, H * HD)).astype(BF16)
    moves[2].wait()
    moves[3].wait()
    for rho, out in enumerate((o0, o1, o2, o3)):
        first = pl.multiple_of((tab[1] ^ rho) * 128, 128)
        out[0:128, 0:HD] = k_ref[pl.ds(first, 128), :]
        out[0:128, HD:] = v_ref[pl.ds(first, 128), :]
        seg = seg_ref[:, pl.ds(first, 128)].astype(F32)
        out[128:, :] = jnp.broadcast_to(jnp.concatenate([seg, seg], axis=1), (16, 256)).astype(BF16)
    moves[4].wait()


def join_body(p0, p1, p2, p3, out):
    row = lax.broadcasted_iota(jnp.int32, (16, 256), 0)
    seg = jnp.zeros((16, 256), F32)
    for rho, part in enumerate((p0, p1, p2, p3)):
        out[128 * rho : 128 * rho + 128, :] = part[0:128, :]
        seg = jnp.where(row == rho, part[128:, :].astype(F32), seg)
    out[NK:, :] = seg.astype(BF16)


def cotangent_body(g_ref, saved_ref, out_ref):
    out_ref[0:NQ, :] = g_ref[...]
    row = lax.broadcasted_iota(jnp.int32, (16, HD), 0)
    for h in range(H):
        cols = slice(h * HD, h * HD + HD)
        both = g_ref[:, cols].astype(F32) * saved_ref[:, cols].astype(F32)
        mean = jnp.sum(both.T, axis=0, keepdims=True)
        top = mean.astype(BF16).astype(F32)
        mid = (mean - top).astype(BF16).astype(F32)
        low = mean - top - mid
        out_ref[NQ:, cols] = jnp.where(row == 0, top, jnp.where(row == 1, mid, low)).astype(BF16)


def turn_body(pieces, q0, q1, q2, q3, tall_ref, wide_ref, row_ref):
    def head(h):
        for rho, q in enumerate((q0, q1, q2, q3)):
            tile = q[0:NQ, lanes(h)]
            tall_ref[rho, lanes(h), :] = tile
            wide_ref[rho, :, lanes(h)] = tile.astype(F32).T.astype(BF16)

    each(H, head)
    for rho, q in enumerate((q0, q1, q2, q3)):
        extra = q[NQ:, :].astype(F32)
        row = extra[0:1, :]
        for n in range(1, pieces):
            row = row + extra[n : n + 1, :]
        row_ref[rho] = row


def item_kind(tab, z_keys, half, rho):
    z, col = tab[0], tab[1]
    own = col ^ rho
    block = 16 * (own >> 1) + 2 * z + (own & 1)
    b0 = col ^ (2 * half)
    b1 = b0 ^ 1
    p0 = (16 * (b0 >> 1) + 2 * z_keys + (b0 & 1)) * NK + 128 * col
    p1 = (16 * (b1 >> 1) + 2 * z_keys + (b1 & 1)) * NK + 128 * col
    first = block * NK + NK - NQ
    full = jnp.maximum(p0, p1) + 127 <= first
    some = jnp.minimum(p0, p1) <= first + NQ - 1 + 1023
    return p0, p1, first, full, some


def visible_of(kv, n, half, p0, p1, first, tag):
    row = lax.broadcasted_iota(jnp.int32, (128, NQ), 0)
    query = lax.broadcasted_iota(jnp.int32, (128, NQ), 1) + first
    seg = kv[n, NK:, 0:128].astype(F32)
    which = lax.broadcasted_iota(jnp.int32, (16, 128), 0)
    parts = []
    for c, p in enumerate((p0, p1)):
        line = jnp.sum(jnp.where(which == 2 * half + c, seg, 0.0), axis=0, keepdims=True)
        parts.append(jnp.where((p + row <= query) | (column(line) == tag), 1.0, 0.0))
    both = jnp.concatenate(parts, axis=0)
    return jnp.concatenate([both, both], axis=1) > 0.5


def items(ks, rhos, tab, body, masks):
    edge = 0 in ks or 1 in ks
    own = ks == (0,)

    def item(t, _):
        n = t // len(rhos)
        rho = rhos[0] + t % len(rhos)
        k = ks[0] if len(ks) == 1 else jnp.where(n == 0, ks[0], ks[1])
        z_keys = (tab[0] + k + NZ) & (NZ - 1)

        def one(half, _):
            kind = item_kind(tab, z_keys, half, rho)
            full, some = kind[3:]
            if edge:
                pl.when(full | some)(lambda: body(n, rho, half, NK // 2, kind, masks))
            else:
                pl.when(full)(lambda: body(n, rho, half, NK // 2, kind, False))
            return 0

        if own:
            lax.fori_loop(0, 2, one, 0)
        else:
            both = item_kind(tab, z_keys, 0, rho)[3] & item_kind(tab, z_keys, 1, rho)[3]
            pl.when(both)(lambda: body(n, rho, 0, NK, None, False))

            @pl.when(jnp.logical_not(both))
            def _():
                lax.fori_loop(0, 2, one, 0)

        return 0

    lax.fori_loop(0, len(rhos) * len(ks), item, 0)


def stats_body(ks, *refs):
    n_sets = len(ks)
    tab, tag_ref, wide_ref = refs[:3]
    kvs = refs[5 : 5 + n_sets]
    m_ref, l_ref, e_ref, t_ref, kv, sum_ref = refs[5 + n_sets :]
    m_ref[...] = refs[3][...]
    l_ref[...] = refs[4][...]
    take_sets(kv, kvs)

    def inputs(n, rho, half, size, kind, masked):
        rows = pl.ds(pl.multiple_of(half * 256, 256), size)
        vis = visible_of(kv, n, half, *kind[:3], tag_ref[rho, :, 0:128]) if masked else None
        return rows, kv[n, rows, 0:HD], vis

    def scores(keys, rho, cols, vis):
        s = dot_nn(keys, wide_ref[rho, :, cols])
        return s if vis is None else jnp.where(vis, s, NEG)

    def first_body(n, rho, half, size, kind, masked):
        rows, keys, vis = inputs(n, rho, half, size, kind, masked)
        for p in range(4):
            cols = slice(256 * p, 256 * p + 256)
            s = scores(keys, rho, cols, vis)
            m_old = m_ref[rho, :, cols]
            m_new = jnp.maximum(m_old, jnp.max(s, axis=0, keepdims=True))
            e = jnp.exp2((s - m_new) * C2)
            if masked:
                e = jnp.where(vis, e, 0.0)
            e_ref[n * 4 + rho, rows, cols] = e.astype(BF16)
            t_ref[(n * 4 + rho) * 2 + half, :, cols] = m_new
            l_ref[rho, :, cols] = l_ref[rho, :, cols] * jnp.exp2((m_old - m_new) * C2) + jnp.sum(
                e, axis=0, keepdims=True
            )
            m_ref[rho, :, cols] = m_new

    def later_body(n, rho, half, size, kind, masked):
        rows, keys, vis = inputs(n, rho, half, size, kind, masked)
        t_ref[(n * 4 + rho) * 2 + half] = m_ref[rho]
        for p in range(4):
            cols = slice(256 * p, 256 * p + 256)
            e = jnp.exp2((scores(keys, rho, cols, vis) - m_ref[rho, :, cols]) * C2)
            e_ref[n * 4 + rho, rows, cols] = e.astype(BF16)
            sum_ref[rho, :, cols] += jnp.sum(e, axis=0, keepdims=True)

    def attempt(_):
        sum_ref[...] = jnp.zeros_like(sum_ref)
        items(ks, (0, 1, 2, 3), tab, later_body, True)
        sums = sum_ref[...]
        step = jnp.where(sums > 2.0**100, 80.0, jnp.where(sums > 2.0**40, 26.0, 0.0))
        m_ref[...] += step * (1.0 / C2)
        return jnp.max(step)

    if ks == (0,):
        items(ks, (0, 1, 2, 3), tab, first_body, True)
    else:
        lax.while_loop(lambda step: step > 0.0, attempt, jnp.float32(1.0))
        l_ref[...] = l_ref[...] * jnp.exp2((refs[3][...] - m_ref[...]) * C2) + sum_ref[...]


def grads_body(ks, rhos, first, last, *refs):
    n_sets = len(ks)
    tab, mean_ref, log_ref, qt_ref, gw_ref, gt_ref, e_ref, t_ref = refs[:8]
    kvs, rest = refs[8 : 8 + n_sets], refs[8 + n_sets :]
    if first:
        dq_ref, acc, kv, p_all, d_all = rest

        def wipe(t):
            dq_ref[:, :, lanes(t)] = jnp.zeros((4, HD, 128), F32)

        each(H, wipe)
    elif last:
        dq_in, o0, o1, acc, kv, p_all, d_all, dq_ref = rest

        def fetch(t):
            dq_ref[:, :, lanes(t)] = dq_in[rhos[0] : rhos[0] + 2, :, lanes(t)]

        each(H, fetch)
    else:
        _, dq_ref, acc, kv, p_all, d_all = rest
    take_sets(kv, kvs)

    def clear(t):
        acc[:, lanes(t), :] = jnp.zeros((n_sets, 128, 2 * HD), F32)

    each(NK // 128, clear)

    def body(n, rho, half, size, kind, masked):
        rows = pl.ds(pl.multiple_of(half * 256, 256), size)
        keys = kv[n, rows, 0:HD]
        vals = kv[n, rows, HD:]
        for p in range(4):
            cols = slice(256 * p, 256 * p + 256)
            dp = dot_nn(vals, gw_ref[rho, :, cols])
            share = jnp.exp2((t_ref[(n * 4 + rho) * 2 + half, :, cols] - log_ref[rho, :, cols]) * C2)
            prob = e_ref[n * 4 + rho, rows, cols].astype(F32) * share
            p_all[0:size, cols] = prob.astype(BF16)
            d_all[0:size, cols] = (prob * (dp - mean_ref[rho, :, cols])).astype(BF16)
        d = d_all[0:size, :]
        acc[n, rows, 0:HD] += dot_nn(d, qt_ref[rho])
        acc[n, rows, HD:] += dot_nn(p_all[0:size, :], gt_ref[rho])
        dq_ref[rho - rhos[0]] += dot_tn(keys, d)

    items(ks, rhos, tab, body, False)
    if last:

        def head(h):
            for r, out in enumerate((o0, o1)):
                out[:, lanes(h)] = (dq_ref[r, :, lanes(h)].T * SCALE).astype(BF16)

        each(H, head)


def place_body(tab, a0, a1, a2, a3, q0, q1, q2, gq_ref, gk_ref, gv_ref):
    col = tab[1]
    for rho, part in enumerate((a0, a1, a2, a3)):
        rows = pl.ds(pl.multiple_of((col ^ rho) * 128, 128), 128)
        gk_ref[rows, :] = part[:, 0:HD]
        gv_ref[rows, :] = part[:, HD:]
    total = q0[...].astype(F32) + q1[...].astype(F32) + q2[...].astype(F32)
    gq_ref[...] = total.astype(BF16)


def per_device(queries, keys, values, grad_out, saved_out, segment_ids, frame_flags):
    hop = functools.partial(lax.ppermute, axis_name="ctx")
    rank = lax.axis_index("ctx").astype(jnp.int32)

    def place_of(rank):
        return jnp.stack([(rank >> 1) & 7, 2 * (rank >> 4) + (rank & 1)])

    tab = place_of(lax.optimization_barrier(rank))
    hbm = pl.BlockSpec(memory_space=pltpu.HBM)

    *parts, q_own = call(
        begin_body, [shape((144, 256))] * 4 + [shape((NQ + 16, H * HD))], [SM] + [hbm] * 5, nbytes=MIB,
        scratch=[
            pltpu.VMEM((NK, HD), BF16), pltpu.VMEM((NK, HD), BF16), pltpu.VMEM((1, NK), jnp.int32),
            pltpu.VMEM((1, 128), jnp.int32), pltpu.SemaphoreType.DMA((5,)),
        ],
        vmem=58,
    )(place_of(rank), keys[0], values[0], segment_ids, frame_flags, queries[0])
    got = [hop(parts[r], perm=flip(r)) for r in (1, 2, 3)]
    own_set = call(join_body, shape((NK + 16, 256)), [VM] * 4, nbytes=MIB)(parts[0], *got)

    def four(x):
        other = hop(x, perm=flip(2))
        last = hop(other, perm=flip(1))
        return (x, hop(x, perm=flip(1)), other, last)

    q_four = four(q_own)
    g_own = call(cotangent_body, shape((NQ + 16, H * HD)), [VM] * 2, nbytes=MIB)(grad_out[0], saved_out[0])
    forms = [shape((4, NQ * H, HD)), shape((4, HD, NQ * H)), shape((4, 1, NQ * H), F32)]

    def turned(four_of, pieces):
        return call(functools.partial(turn_body, pieces), forms, [VM] * 4, vmem=16, nbytes=4 * MIB)(*four_of)

    q_tall, q_wide, tag = turned(q_four, 1)
    stat = shape((4, 1, NQ * H), F32)
    m = jnp.full((4, 1, NQ * H), NEG, F32)
    l = jnp.zeros((4, 1, NQ * H), F32)
    sets = {0: own_set}
    kept = {}
    fwd = bwd = own_set
    for step in range(5):
        ks = (0,) if step == 0 else (4,) if step == 4 else (step, -step)
        n = len(ks)
        if step < 3:
            fwd, bwd = hop(fwd, perm=turn(1)), hop(bwd, perm=turn(-1))
        elif step == 3:
            bwd = hop(bwd, perm=turn(-1))
        m, l, *kept[ks] = call(
            functools.partial(stats_body, ks),
            [stat, stat, shape((4 * n, NK, NQ * H)), shape((8 * n, 1, NQ * H), F32)],
            [SM] + [VM] * (4 + n), vmem=3,
            scratch=[pltpu.VMEM((n, NK + 16, 256), BF16)] + [pltpu.VMEM((4, 1, NQ * H), F32)],
            flops=n * (1 << 29), nbytes=2 * MIB,
        )(tab, tag, q_wide, m, l, *[sets[k] for k in ks])
        if step < 4:
            if step > 0:
                fwd, bwd, m, l = lax.optimization_barrier((fwd, bwd, m, l))
            sets[step + 1] = bwd
            if step < 3:
                sets[-step - 1] = fwd
        if step == 0:
            g_four = four(g_own)
    g_tall, g_wide, mean = turned(g_four, 3)

    ml = jnp.concatenate([m, l], axis=0)
    tops, sums = [m], [l]
    for r in (1, 2, 3):
        got = hop(ml, perm=flip(r))
        tops.append(jnp.concatenate([got[rho ^ r : (rho ^ r) + 1] for rho in range(4)], axis=0))
        sums.append(jnp.concatenate([got[4 + (rho ^ r) : 5 + (rho ^ r)] for rho in range(4)], axis=0))
    top = functools.reduce(jnp.maximum, tops)
    total = sum(s * jnp.exp2((t - top) * C2) for s, t in zip(sums, tops))
    log_total = top + jnp.log2(total) * (1.0 / C2)

    dq = None
    up = down = None
    dq_shape = shape((4, HD, NQ * H), F32)

    def grads(ks, rhos, dq):
        n = len(ks)
        first, last = dq is None, ks == (0,)
        args = [tab, mean, log_total, q_tall, g_wide, g_tall, *kept[ks]] + [sets[k] for k in ks]
        args += [] if first else [dq]
        piece = shape((NQ, H * HD))
        scratch = [pltpu.VMEM((n, NK + 16, 256), BF16)] + [pltpu.VMEM((NK, NQ * H), BF16)] * 2
        return call(
            functools.partial(grads_body, ks, rhos, first, last),
            ([piece, piece] if last else [dq_shape]) + [shape((n, NK, 2 * HD), F32)],
            [SM] + [VM] * (len(args) - 1),
            scratch=scratch + ([pltpu.VMEM((2, HD, NQ * H), F32)] if last else []),
            vmem=5, flops=n * 5 * (1 << 29), nbytes=8 * MIB,
            alias={} if first or last else {len(args) - 1: 0},
        )(*args)

    for ks in ((4,), (3, -3), (2, -2), (1, -1)):
        n = len(ks)
        dq, adds = grads(ks, (0, 1, 2, 3), dq)
        sends = [(adds[0] if up is None else adds[0] + up.astype(F32)).astype(BF16)]
        if n == 2:
            sends.append((adds[1] if down is None else adds[1] + down.astype(F32)).astype(BF16))
        dq, *sends = lax.optimization_barrier((dq, *sends))
        up = hop(sends[0], perm=turn(1))
        if n == 2:
            down = hop(sends[1], perm=turn(-1))
    dq2, dq3, far_adds = grads((0,), (2, 3), dq)
    dq3 = hop(dq3, perm=flip(1))
    across = (dq2.astype(F32) + dq3.astype(F32)).astype(BF16)
    dq_far = hop(across, perm=flip(2))
    dq0, dq1, near_adds = grads((0,), (0, 1), dq)
    own = far_adds[0] + near_adds[0] + up.astype(F32) + down.astype(F32)
    scales = jnp.where(jnp.arange(2 * HD) < HD, SCALE, 1.0).astype(F32)
    own = (own * scales[None, :]).astype(BF16)
    q_back = [dq0, hop(dq1, perm=flip(1)), dq_far]
    a_back = [own[0:128]] + [hop(own[128 * r : 128 * r + 128], perm=flip(r)) for r in (1, 2, 3)]
    gq, gk, gv = call(
        place_body, [shape((NQ, H * HD)), shape((NK, HD)), shape((NK, HD))], [SM] + [VM] * 7,
        nbytes=2 * MIB,
    )(tab, *a_back, *q_back)
    return gq[None], gk[None], gv[None]


def solution(mesh):
    row = P("dp", "ctx", None)
    return jax.shard_map(
        per_device,
        mesh=mesh,
        in_specs=(row, row, row, row, row, P("dp", "ctx"), P("dp", None)),
        out_specs=(row, row, row),
        check_vma=False,
    )
```

```python
import functools
import math

import jax
import jax.numpy as jnp
from jax import lax
from jax.experimental import pallas as pl
from jax.experimental.pallas import tpu as pltpu
from jax.sharding import PartitionSpec as P


H = 8
HD = 128
NQ = 128
NK = 512
NZ = 8
SCALE = 1.0 / math.sqrt(HD)
C2 = SCALE * math.log2(math.e)
NEG = -1e30
F32 = jnp.float32
BF16 = jnp.bfloat16
VM = pl.BlockSpec(memory_space=pltpu.VMEM)
SM = pl.BlockSpec(memory_space=pltpu.SMEM)
MIB = 1 << 20


def flip(rho):
    mask = (rho & 1) | ((rho >> 1) << 4)
    return [(i, i ^ mask) for i in range(32)]


def turn(step):
    return [(i, (i // 16) * 16 + (i % 16 + 2 * step) % 16) for i in range(32)]


def dot_nn(left, right):
    return lax.dot_general(left, right, (((1,), (0,)), ((), ())), preferred_element_type=F32)


def dot_tn(left, right):
    return lax.dot_general(left, right, (((0,), (0,)), ((), ())), preferred_element_type=F32)


def call(body, out, specs, scratch=(), vmem=8, flops=0, nbytes=0, alias=None):
    return pl.pallas_call(
        body,
        out_shape=out,
        in_specs=specs,
        out_specs=jax.tree.map(lambda _: VM, out),
        scratch_shapes=list(scratch),
        input_output_aliases=alias or {},
        cost_estimate=pl.CostEstimate(flops=flops, bytes_accessed=nbytes, transcendentals=0),
        compiler_params=pltpu.CompilerParams(vmem_limit_bytes=vmem * MIB),
    )


def shape(dims, dtype=BF16):
    return jax.ShapeDtypeStruct(dims, dtype)


def each(count, body):
    lax.fori_loop(0, count, lambda t, _: (body(t), 0)[1], 0)


def lanes(t):
    return pl.ds(pl.multiple_of(t * 128, 128), 128)


def take_sets(kv, kvs):
    def rows(t):
        part = pl.ds(pl.multiple_of(t * 48, 16), 48)
        for n in range(len(kvs)):
            kv[n, part, :] = kvs[n][part, :]

    each(11, rows)


def column(row):
    return jnp.broadcast_to(row, (128, 128)).T


def begin_body(tab, k_hbm, v_hbm, seg_hbm, flag_hbm, q_hbm, o0, o1, o2, o3, q_out, k_ref, v_ref, seg_ref, flag_ref, sems):
    moves = [
        pltpu.make_async_copy(source, target, sems.at[n])
        for n, (source, target) in enumerate(
            [(seg_hbm, seg_ref), (flag_hbm, flag_ref), (k_hbm, k_ref), (v_hbm, v_ref), (q_hbm, q_out.at[0:NQ, :])]
        )
    ]
    for move in moves:
        move.start()
    moves[0].wait()
    moves[1].wait()
    own = seg_ref[:, NK - NQ :]
    ident = lax.broadcasted_iota(jnp.int32, (128, 128), 0)
    framed = jnp.sum(jnp.where(ident == own, column(flag_ref[...]), 0), axis=0, keepdims=True)
    tag = jnp.where(framed == 1, own, -1).astype(F32)
    q_out[NQ:, :] = jnp.broadcast_to(jnp.concatenate([tag] * H, axis=1), (16, H * HD)).astype(BF16)
    moves[2].wait()
    moves[3].wait()
    for rho, out in enumerate((o0, o1, o2, o3)):
        first = pl.multiple_of((tab[1] ^ rho) * 128, 128)
        out[0:128, 0:HD] = k_ref[pl.ds(first, 128), :]
        out[0:128, HD:] = v_ref[pl.ds(first, 128), :]
        seg = seg_ref[:, pl.ds(first, 128)].astype(F32)
        out[128:, :] = jnp.broadcast_to(jnp.concatenate([seg, seg], axis=1), (16, 256)).astype(BF16)
    moves[4].wait()


def join_body(p0, p1, p2, p3, out):
    row = lax.broadcasted_iota(jnp.int32, (16, 256), 0)
    seg = jnp.zeros((16, 256), F32)
    for rho, part in enumerate((p0, p1, p2, p3)):
        out[128 * rho : 128 * rho + 128, :] = part[0:128, :]
        seg = jnp.where(row == rho, part[128:, :].astype(F32), seg)
    out[NK:, :] = seg.astype(BF16)


def cotangent_body(g_ref, saved_ref, out_ref):
    out_ref[0:NQ, :] = g_ref[...]
    row = lax.broadcasted_iota(jnp.int32, (16, HD), 0)
    for h in range(H):
        cols = slice(h * HD, h * HD + HD)
        both = g_ref[:, cols].astype(F32) * saved_ref[:, cols].astype(F32)
        mean = jnp.sum(both.T, axis=0, keepdims=True)
        top = mean.astype(BF16).astype(F32)
        mid = (mean - top).astype(BF16).astype(F32)
        low = mean - top - mid
        out_ref[NQ:, cols] = jnp.where(row == 0, top, jnp.where(row == 1, mid, low)).astype(BF16)


def turn_body(pieces, q0, q1, q2, q3, tall_ref, wide_ref, row_ref):
    def head(h):
        for rho, q in enumerate((q0, q1, q2, q3)):
            tile = q[0:NQ, lanes(h)]
            tall_ref[rho, lanes(h), :] = tile
            wide_ref[rho, :, lanes(h)] = tile.astype(F32).T.astype(BF16)

    each(H, head)
    for rho, q in enumerate((q0, q1, q2, q3)):
        extra = q[NQ:, :].astype(F32)
        row = extra[0:1, :]
        for n in range(1, pieces):
            row = row + extra[n : n + 1, :]
        row_ref[rho] = row


def item_kind(tab, z_keys, half, rho):
    z, col = tab[0], tab[1]
    own = col ^ rho
    block = 16 * (own >> 1) + 2 * z + (own & 1)
    b0 = col ^ (2 * half)
    b1 = b0 ^ 1
    p0 = (16 * (b0 >> 1) + 2 * z_keys + (b0 & 1)) * NK + 128 * col
    p1 = (16 * (b1 >> 1) + 2 * z_keys + (b1 & 1)) * NK + 128 * col
    first = block * NK + NK - NQ
    full = jnp.maximum(p0, p1) + 127 <= first
    some = jnp.minimum(p0, p1) <= first + NQ - 1 + 1023
    return p0, p1, first, full, some


def visible_of(kv, n, half, p0, p1, first, tag):
    row = lax.broadcasted_iota(jnp.int32, (128, NQ), 0)
    query = lax.broadcasted_iota(jnp.int32, (128, NQ), 1) + first
    seg = kv[n, NK:, 0:128].astype(F32)
    which = lax.broadcasted_iota(jnp.int32, (16, 128), 0)
    parts = []
    for c, p in enumerate((p0, p1)):
        line = jnp.sum(jnp.where(which == 2 * half + c, seg, 0.0), axis=0, keepdims=True)
        parts.append(jnp.where((p + row <= query) | (column(line) == tag), 1.0, 0.0))
    both = jnp.concatenate(parts, axis=0)
    return jnp.concatenate([both, both], axis=1) > 0.5


def items(ks, rhos, tab, tag_ref, kv, body, masks):
    edge = 0 in ks or 1 in ks
    own = ks == (0,)

    def item(t, _):
        n = t // len(rhos)
        rho = rhos[0] + t % len(rhos)
        k = ks[0] if len(ks) == 1 else jnp.where(n == 0, ks[0], ks[1])
        z_keys = (tab[0] + k + NZ) & (NZ - 1)

        def one(half, _):
            kind = item_kind(tab, z_keys, half, rho)
            p0, p1, first, full, some = kind
            if edge:

                def framed():
                    which = lax.broadcasted_iota(jnp.int32, (16, 128), 0) >> 1
                    least = jnp.min(jnp.where(which == half, kv[n, NK:, 0:128].astype(F32), 1e9))
                    return (least <= jnp.max(tag_ref[rho, :, 0:128])).astype(jnp.int32)

                past = jnp.minimum(p0, p1) > first + NQ - 1
                some = some & (lax.cond(some & past, framed, lambda: jnp.int32(1)) > 0)
                pl.when(full | some)(lambda: body(n, rho, half, NK // 2, kind, masks))
            else:
                pl.when(full)(lambda: body(n, rho, half, NK // 2, kind, False))
            return 0

        if own:
            lax.fori_loop(0, 2, one, 0)
        else:
            both = item_kind(tab, z_keys, 0, rho)[3] & item_kind(tab, z_keys, 1, rho)[3]
            pl.when(both)(lambda: body(n, rho, 0, NK, None, False))

            @pl.when(jnp.logical_not(both))
            def _():
                lax.fori_loop(0, 2, one, 0)

        return 0

    lax.fori_loop(0, len(rhos) * len(ks), item, 0)


def stats_body(ks, *refs):
    n_sets = len(ks)
    tab, tag_ref, wide_ref = refs[:3]
    kvs = refs[5 : 5 + n_sets]
    m_ref, l_ref, e_ref, t_ref, kv, sum_ref = refs[5 + n_sets :]
    m_ref[...] = refs[3][...]
    l_ref[...] = refs[4][...]
    take_sets(kv, kvs)

    def inputs(n, rho, half, size, kind, masked):
        rows = pl.ds(pl.multiple_of(half * 256, 256), size)
        vis = visible_of(kv, n, half, *kind[:3], tag_ref[rho, :, 0:128]) if masked else None
        return rows, kv[n, rows, 0:HD], vis

    def scores(keys, rho, cols, vis):
        s = dot_nn(keys, wide_ref[rho, :, cols])
        return s if vis is None else jnp.where(vis, s, NEG)

    def first_body(n, rho, half, size, kind, masked):
        rows, keys, vis = inputs(n, rho, half, size, kind, masked)
        for p in range(4):
            cols = slice(256 * p, 256 * p + 256)
            s = scores(keys, rho, cols, vis)
            m_old = m_ref[rho, :, cols]
            m_new = jnp.maximum(m_old, jnp.max(s, axis=0, keepdims=True))
            e = jnp.exp2((s - m_new) * C2)
            if masked:
                e = jnp.where(vis, e, 0.0)
            e_ref[n * 4 + rho, rows, cols] = e.astype(BF16)
            t_ref[(n * 4 + rho) * 2 + half, :, cols] = m_new
            l_ref[rho, :, cols] = l_ref[rho, :, cols] * jnp.exp2((m_old - m_new) * C2) + jnp.sum(
                e, axis=0, keepdims=True
            )
            m_ref[rho, :, cols] = m_new

    def later_body(n, rho, half, size, kind, masked):
        rows, keys, vis = inputs(n, rho, half, size, kind, masked)
        t_ref[(n * 4 + rho) * 2 + half] = m_ref[rho]
        for p in range(4):
            cols = slice(256 * p, 256 * p + 256)
            e = jnp.exp2((scores(keys, rho, cols, vis) - m_ref[rho, :, cols]) * C2)
            e_ref[n * 4 + rho, rows, cols] = e.astype(BF16)
            sum_ref[rho, :, cols] += jnp.sum(e, axis=0, keepdims=True)

    def attempt(_):
        sum_ref[...] = jnp.zeros_like(sum_ref)
        items(ks, (0, 1, 2, 3), tab, tag_ref, kv, later_body, True)
        sums = sum_ref[...]
        step = jnp.where(sums > 2.0**100, 80.0, jnp.where(sums > 2.0**40, 26.0, 0.0))
        m_ref[...] += step * (1.0 / C2)
        return jnp.max(step)

    if ks == (0,):
        items(ks, (0, 1, 2, 3), tab, tag_ref, kv, first_body, True)
    else:
        lax.while_loop(lambda step: step > 0.0, attempt, jnp.float32(1.0))
        l_ref[...] = l_ref[...] * jnp.exp2((refs[3][...] - m_ref[...]) * C2) + sum_ref[...]


def grads_body(ks, rhos, first, last, *refs):
    n_sets = len(ks)
    tab, tag_ref, mean_ref, log_ref, qt_ref, gw_ref, gt_ref, e_ref, t_ref = refs[:9]
    kvs, rest = refs[9 : 9 + n_sets], refs[9 + n_sets :]
    if first:
        dq_ref, acc, kv, p_all, d_all = rest

        def wipe(t):
            dq_ref[:, :, lanes(t)] = jnp.zeros((4, HD, 128), F32)

        each(H, wipe)
    elif last:
        dq_in, o0, o1, acc, kv, p_all, d_all, dq_ref = rest

        def fetch(t):
            dq_ref[:, :, lanes(t)] = dq_in[rhos[0] : rhos[0] + 2, :, lanes(t)]

        each(H, fetch)
    else:
        _, dq_ref, acc, kv, p_all, d_all = rest
    take_sets(kv, kvs)

    def clear(t):
        acc[:, lanes(t), :] = jnp.zeros((n_sets, 128, 2 * HD), F32)

    each(NK // 128, clear)

    def body(n, rho, half, size, kind, masked):
        rows = pl.ds(pl.multiple_of(half * 256, 256), size)
        keys = kv[n, rows, 0:HD]
        vals = kv[n, rows, HD:]
        for p in range(4):
            cols = slice(256 * p, 256 * p + 256)
            dp = dot_nn(vals, gw_ref[rho, :, cols])
            share = jnp.exp2((t_ref[(n * 4 + rho) * 2 + half, :, cols] - log_ref[rho, :, cols]) * C2)
            prob = e_ref[n * 4 + rho, rows, cols].astype(F32) * share
            p_all[0:size, cols] = prob.astype(BF16)
            d_all[0:size, cols] = (prob * (dp - mean_ref[rho, :, cols])).astype(BF16)
        d = d_all[0:size, :]
        acc[n, rows, 0:HD] += dot_nn(d, qt_ref[rho])
        acc[n, rows, HD:] += dot_nn(p_all[0:size, :], gt_ref[rho])
        dq_ref[rho - rhos[0]] += dot_tn(keys, d)

    items(ks, rhos, tab, tag_ref, kv, body, False)
    if last:

        def head(h):
            for r, out in enumerate((o0, o1)):
                out[:, lanes(h)] = (dq_ref[r, :, lanes(h)].T * SCALE).astype(BF16)

        each(H, head)


def place_body(tab, a0, a1, a2, a3, q0, q1, q2, gq_ref, gk_ref, gv_ref):
    col = tab[1]
    for rho, part in enumerate((a0, a1, a2, a3)):
        rows = pl.ds(pl.multiple_of((col ^ rho) * 128, 128), 128)
        gk_ref[rows, :] = part[:, 0:HD]
        gv_ref[rows, :] = part[:, HD:]
    total = q0[...].astype(F32) + q1[...].astype(F32) + q2[...].astype(F32)
    gq_ref[...] = total.astype(BF16)


def per_device(queries, keys, values, grad_out, saved_out, segment_ids, frame_flags):
    hop = functools.partial(lax.ppermute, axis_name="ctx")
    rank = lax.axis_index("ctx").astype(jnp.int32)

    def place_of(rank):
        return jnp.stack([(rank >> 1) & 7, 2 * (rank >> 4) + (rank & 1)])

    tab = place_of(lax.optimization_barrier(rank))
    hbm = pl.BlockSpec(memory_space=pltpu.HBM)

    *parts, q_own = call(
        begin_body, [shape((144, 256))] * 4 + [shape((NQ + 16, H * HD))], [SM] + [hbm] * 5, nbytes=MIB,
        scratch=[
            pltpu.VMEM((NK, HD), BF16), pltpu.VMEM((NK, HD), BF16), pltpu.VMEM((1, NK), jnp.int32),
            pltpu.VMEM((1, 128), jnp.int32), pltpu.SemaphoreType.DMA((5,)),
        ],
        vmem=58,
    )(place_of(rank), keys[0], values[0], segment_ids, frame_flags, queries[0])
    got = [hop(parts[r], perm=flip(r)) for r in (1, 2, 3)]
    own_set = call(join_body, shape((NK + 16, 256)), [VM] * 4, nbytes=MIB)(parts[0], *got)

    def four(x):
        other = hop(x, perm=flip(2))
        last = hop(other, perm=flip(1))
        return (x, hop(x, perm=flip(1)), other, last)

    q_four = four(q_own)
    g_own = call(cotangent_body, shape((NQ + 16, H * HD)), [VM] * 2, nbytes=MIB)(grad_out[0], saved_out[0])
    forms = [shape((4, NQ * H, HD)), shape((4, HD, NQ * H)), shape((4, 1, NQ * H), F32)]

    def turned(four_of, pieces):
        return call(functools.partial(turn_body, pieces), forms, [VM] * 4, vmem=16, nbytes=4 * MIB)(*four_of)

    q_tall, q_wide, tag = turned(q_four, 1)
    stat = shape((4, 1, NQ * H), F32)
    m = jnp.full((4, 1, NQ * H), NEG, F32)
    l = jnp.zeros((4, 1, NQ * H), F32)
    sets = {0: own_set}
    kept = {}
    fwd = bwd = own_set
    for step in range(5):
        ks = (0,) if step == 0 else (4,) if step == 4 else (step, -step)
        n = len(ks)
        if step < 3:
            fwd, bwd = hop(fwd, perm=turn(1)), hop(bwd, perm=turn(-1))
        elif step == 3:
            low, high = hop(fwd[0:272], perm=turn(1)), hop(bwd[272:], perm=turn(-1))
            fwd, bwd = low, high
        m, l, *kept[ks] = call(
            functools.partial(stats_body, ks),
            [stat, stat, shape((4 * n, NK, NQ * H)), shape((8 * n, 1, NQ * H), F32)],
            [SM] + [VM] * (4 + n), vmem=3,
            scratch=[pltpu.VMEM((n, NK + 16, 256), BF16)] + [pltpu.VMEM((4, 1, NQ * H), F32)],
            flops=n * (1 << 29), nbytes=2 * MIB,
        )(tab, tag, q_wide, m, l, *[sets[k] for k in ks])
        if step < 4:
            if step > 0:
                fwd, bwd, m, l = lax.optimization_barrier((fwd, bwd, m, l))
            if step < 3:
                sets[step + 1], sets[-step - 1] = bwd, fwd
            else:
                sets[4] = jnp.concatenate([fwd, bwd], axis=0)
        if step == 0:
            g_four = four(g_own)
    g_tall, g_wide, mean = turned(g_four, 3)

    ml = jnp.concatenate([m, l], axis=0)
    tops, sums = [m], [l]
    for r in (1, 2, 3):
        got = hop(ml, perm=flip(r))
        tops.append(jnp.concatenate([got[rho ^ r : (rho ^ r) + 1] for rho in range(4)], axis=0))
        sums.append(jnp.concatenate([got[4 + (rho ^ r) : 5 + (rho ^ r)] for rho in range(4)], axis=0))
    top = functools.reduce(jnp.maximum, tops)
    total = sum(s * jnp.exp2((t - top) * C2) for s, t in zip(sums, tops))
    log_total = top + jnp.log2(total) * (1.0 / C2)

    dq = None
    up = down = None
    dq_shape = shape((4, HD, NQ * H), F32)

    def grads(ks, rhos, dq):
        n = len(ks)
        first, last = dq is None, ks == (0,)
        args = [tab, tag, mean, log_total, q_tall, g_wide, g_tall, *kept[ks]] + [sets[k] for k in ks]
        args += [] if first else [dq]
        piece = shape((NQ, H * HD))
        scratch = [pltpu.VMEM((n, NK + 16, 256), BF16)] + [pltpu.VMEM((NK, NQ * H), BF16)] * 2
        return call(
            functools.partial(grads_body, ks, rhos, first, last),
            ([piece, piece] if last else [dq_shape]) + [shape((n, NK, 2 * HD), F32)],
            [SM] + [VM] * (len(args) - 1),
            scratch=scratch + ([pltpu.VMEM((2, HD, NQ * H), F32)] if last else []),
            vmem=5, flops=n * 5 * (1 << 29), nbytes=8 * MIB,
            alias={} if first or last else {len(args) - 1: 0},
        )(*args)

    for ks in ((4,), (3, -3), (2, -2), (1, -1)):
        n = len(ks)
        dq, adds = grads(ks, (0, 1, 2, 3), dq)
        sends = [(adds[0] if up is None else adds[0] + up.astype(F32)).astype(BF16)]
        if n == 2:
            sends.append((adds[1] if down is None else adds[1] + down.astype(F32)).astype(BF16))
        dq, *sends = lax.optimization_barrier((dq, *sends))
        up = hop(sends[0], perm=turn(1))
        if n == 2:
            down = hop(sends[1], perm=turn(-1))
    dq2, dq3, far_adds = grads((0,), (2, 3), dq)
    dq3 = hop(dq3, perm=flip(1))
    across = (dq2.astype(F32) + dq3.astype(F32)).astype(BF16)
    dq_far = hop(across, perm=flip(2))
    dq0, dq1, near_adds = grads((0,), (0, 1), dq)
    own = far_adds[0] + near_adds[0] + up.astype(F32) + down.astype(F32)
    scales = jnp.where(jnp.arange(2 * HD) < HD, SCALE, 1.0).astype(F32)
    own = (own * scales[None, :]).astype(BF16)
    q_back = [dq0, hop(dq1, perm=flip(1)), dq_far]
    a_back = [own[0:128]] + [hop(own[128 * r : 128 * r + 128], perm=flip(r)) for r in (1, 2, 3)]
    gq, gk, gv = call(
        place_body, [shape((NQ, H * HD)), shape((NK, HD)), shape((NK, HD))], [SM] + [VM] * 7,
        nbytes=2 * MIB,
    )(tab, *a_back, *q_back)
    return gq[None], gk[None], gv[None]


def solution(mesh):
    row = P("dp", "ctx", None)
    return jax.shard_map(
        per_device,
        mesh=mesh,
        in_specs=(row, row, row, row, row, P("dp", "ctx"), P("dp", None)),
        out_specs=(row, row, row),
        check_vma=False,
    )
```

```python
import functools
import math

import jax
import jax.numpy as jnp
from jax import lax
from jax.experimental import pallas as pl
from jax.experimental.pallas import tpu as pltpu
from jax.sharding import PartitionSpec as P


H = 8
HD = 128
NQ = 128
NK = 512
NZ = 8
SCALE = 1.0 / math.sqrt(HD)
C2 = SCALE * math.log2(math.e)
NEG = -1e30
F32 = jnp.float32
BF16 = jnp.bfloat16
VM = pl.BlockSpec(memory_space=pltpu.VMEM)
SM = pl.BlockSpec(memory_space=pltpu.SMEM)
MIB = 1 << 20


def flip(rho):
    mask = (rho & 1) | ((rho >> 1) << 4)
    return [(i, i ^ mask) for i in range(32)]


def turn(step):
    return [(i, (i // 16) * 16 + (i % 16 + 2 * step) % 16) for i in range(32)]


def dot_nn(left, right):
    return lax.dot_general(left, right, (((1,), (0,)), ((), ())), preferred_element_type=F32)


def dot_tn(left, right):
    return lax.dot_general(left, right, (((0,), (0,)), ((), ())), preferred_element_type=F32)


def call(body, out, specs, scratch=(), vmem=8, flops=0, nbytes=0, alias=None):
    return pl.pallas_call(
        body,
        out_shape=out,
        in_specs=specs,
        out_specs=jax.tree.map(lambda _: VM, out),
        scratch_shapes=list(scratch),
        input_output_aliases=alias or {},
        cost_estimate=pl.CostEstimate(flops=flops, bytes_accessed=nbytes, transcendentals=0),
        compiler_params=pltpu.CompilerParams(vmem_limit_bytes=vmem * MIB),
    )


def shape(dims, dtype=BF16):
    return jax.ShapeDtypeStruct(dims, dtype)


def each(count, body):
    lax.fori_loop(0, count, lambda t, _: (body(t), 0)[1], 0)


def lanes(t):
    return pl.ds(pl.multiple_of(t * 128, 128), 128)


def take_sets(kv, kvs):
    def rows(t):
        part = pl.ds(pl.multiple_of(t * 48, 16), 48)
        for n in range(len(kvs)):
            kv[n, part, :] = kvs[n][part, :]

    each(11, rows)


def column(row):
    return jnp.broadcast_to(row, (128, 128)).T


def begin_body(tab, k_hbm, v_hbm, seg_hbm, flag_hbm, q_hbm, o0, o1, o2, o3, q_out, k_ref, v_ref, seg_ref, flag_ref, sems):
    moves = [
        pltpu.make_async_copy(source, target, sems.at[n])
        for n, (source, target) in enumerate(
            [(seg_hbm, seg_ref), (flag_hbm, flag_ref), (k_hbm, k_ref), (v_hbm, v_ref), (q_hbm, q_out.at[0:NQ, :])]
        )
    ]
    for move in moves:
        move.start()
    moves[0].wait()
    moves[1].wait()
    own = seg_ref[:, NK - NQ :]
    ident = lax.broadcasted_iota(jnp.int32, (128, 128), 0)
    framed = jnp.sum(jnp.where(ident == own, column(flag_ref[...]), 0), axis=0, keepdims=True)
    tag = jnp.where(framed == 1, own, -1).astype(F32)
    q_out[NQ:, :] = jnp.broadcast_to(jnp.concatenate([tag] * H, axis=1), (16, H * HD)).astype(BF16)
    moves[2].wait()
    moves[3].wait()
    for rho, out in enumerate((o0, o1, o2, o3)):
        first = pl.multiple_of((tab[1] ^ rho) * 128, 128)
        out[0:128, 0:HD] = k_ref[pl.ds(first, 128), :]
        out[0:128, HD:] = v_ref[pl.ds(first, 128), :]
        seg = seg_ref[:, pl.ds(first, 128)].astype(F32)
        out[128:, :] = jnp.broadcast_to(jnp.concatenate([seg, seg], axis=1), (16, 256)).astype(BF16)
    moves[4].wait()


def join_body(p0, p1, p2, p3, out):
    row = lax.broadcasted_iota(jnp.int32, (16, 256), 0)
    seg = jnp.zeros((16, 256), F32)
    for rho, part in enumerate((p0, p1, p2, p3)):
        out[128 * rho : 128 * rho + 128, :] = part[0:128, :]
        seg = jnp.where(row == rho, part[128:, :].astype(F32), seg)
    out[NK:, :] = seg.astype(BF16)


def cotangent_body(g_ref, saved_ref, out_ref):
    out_ref[0:NQ, :] = g_ref[...]
    row = lax.broadcasted_iota(jnp.int32, (16, HD), 0)
    for h in range(H):
        cols = slice(h * HD, h * HD + HD)
        both = g_ref[:, cols].astype(F32) * saved_ref[:, cols].astype(F32)
        mean = jnp.sum(both.T, axis=0, keepdims=True)
        top = mean.astype(BF16).astype(F32)
        mid = (mean - top).astype(BF16).astype(F32)
        low = mean - top - mid
        out_ref[NQ:, cols] = jnp.where(row == 0, top, jnp.where(row == 1, mid, low)).astype(BF16)


def turn_body(pieces, q0, q1, q2, q3, tall_ref, wide_ref, row_ref):
    def head(h):
        for rho, q in enumerate((q0, q1, q2, q3)):
            tile = q[0:NQ, lanes(h)]
            tall_ref[rho, lanes(h), :] = tile
            wide_ref[rho, :, lanes(h)] = tile.astype(F32).T.astype(BF16)

    each(H, head)
    for rho, q in enumerate((q0, q1, q2, q3)):
        extra = q[NQ:, :].astype(F32)
        row = extra[0:1, :]
        for n in range(1, pieces):
            row = row + extra[n : n + 1, :]
        row_ref[rho] = row


def item_kind(tab, z_keys, half, rho):
    z, col = tab[0], tab[1]
    own = col ^ rho
    block = 16 * (own >> 1) + 2 * z + (own & 1)
    b0 = col ^ (2 * half)
    b1 = b0 ^ 1
    p0 = (16 * (b0 >> 1) + 2 * z_keys + (b0 & 1)) * NK + 128 * col
    p1 = (16 * (b1 >> 1) + 2 * z_keys + (b1 & 1)) * NK + 128 * col
    first = block * NK + NK - NQ
    full = jnp.maximum(p0, p1) + 127 <= first
    some = jnp.minimum(p0, p1) <= first + NQ - 1 + 1023
    return p0, p1, first, full, some


def visible_of(kv, n, half, p0, p1, first, tag):
    row = lax.broadcasted_iota(jnp.int32, (128, NQ), 0)
    query = lax.broadcasted_iota(jnp.int32, (128, NQ), 1) + first
    seg = kv[n, NK:, 0:128].astype(F32)
    which = lax.broadcasted_iota(jnp.int32, (16, 128), 0)
    parts = []
    for c, p in enumerate((p0, p1)):
        line = jnp.sum(jnp.where(which == 2 * half + c, seg, 0.0), axis=0, keepdims=True)
        parts.append(jnp.where((p + row <= query) | (column(line) == tag), 1.0, 0.0))
    both = jnp.concatenate(parts, axis=0)
    return jnp.concatenate([both, both], axis=1) > 0.5


def items(ks, rhos, tab, tag_ref, kv, body, masks, wide=True):
    edge = 0 in ks or 1 in ks

    def item(t, _):
        n = t // len(rhos)
        rho = rhos[0] + t % len(rhos)
        k = ks[0] if len(ks) == 1 else jnp.where(n == 0, ks[0], ks[1])
        z_keys = (tab[0] + k + NZ) & (NZ - 1)

        def one(half, _):
            kind = item_kind(tab, z_keys, half, rho)
            p0, p1, first, full, some = kind
            if edge:

                def framed():
                    which = lax.broadcasted_iota(jnp.int32, (16, 128), 0) >> 1
                    least = jnp.min(jnp.where(which == half, kv[n, NK:, 0:128].astype(F32), 1e9))
                    return (least <= jnp.max(tag_ref[rho, :, 0:128])).astype(jnp.int32)

                past = jnp.minimum(p0, p1) > first + NQ - 1
                some = some & (lax.cond(some & past, framed, lambda: jnp.int32(1)) > 0)
                pl.when(full | some)(lambda: body(n, rho, half, NK // 2, kind, masks))
            else:
                pl.when(full)(lambda: body(n, rho, half, NK // 2, kind, False))
            return 0

        if not wide:
            lax.fori_loop(0, 2, one, 0)
        else:
            both = item_kind(tab, z_keys, 0, rho)[3] & item_kind(tab, z_keys, 1, rho)[3]
            pl.when(both)(lambda: body(n, rho, 0, NK, None, False))

            @pl.when(jnp.logical_not(both))
            def _():
                lax.fori_loop(0, 2, one, 0)

        return 0

    lax.fori_loop(0, len(rhos) * len(ks), item, 0)


def stats_body(ks, *refs):
    n_sets = len(ks)
    tab, tag_ref, wide_ref = refs[:3]
    kvs = refs[5 : 5 + n_sets]
    m_ref, l_ref, e_ref, t_ref, kv, sum_ref = refs[5 + n_sets :]
    m_ref[...] = refs[3][...]
    l_ref[...] = refs[4][...]
    take_sets(kv, kvs)

    def inputs(n, rho, half, size, kind, masked):
        rows = pl.ds(pl.multiple_of(half * 256, 256), size)
        vis = visible_of(kv, n, half, *kind[:3], tag_ref[rho, :, 0:128]) if masked else None
        return rows, kv[n, rows, 0:HD], vis

    def scores(keys, rho, cols, vis):
        s = dot_nn(keys, wide_ref[rho, :, cols])
        return s if vis is None else jnp.where(vis, s, NEG)

    def first_body(n, rho, half, size, kind, masked):
        rows, keys, vis = inputs(n, rho, half, size, kind, masked)
        for p in range(4):
            cols = slice(256 * p, 256 * p + 256)
            s = scores(keys, rho, cols, vis)
            m_old = m_ref[rho, :, cols]
            m_new = jnp.maximum(m_old, jnp.max(s, axis=0, keepdims=True))
            e = jnp.exp2((s - m_new) * C2)
            if masked:
                e = jnp.where(vis, e, 0.0)
            e_ref[n * 4 + rho, rows, cols] = e.astype(BF16)
            t_ref[(n * 4 + rho) * 2 + half, :, cols] = m_new
            l_ref[rho, :, cols] = l_ref[rho, :, cols] * jnp.exp2((m_old - m_new) * C2) + jnp.sum(
                e, axis=0, keepdims=True
            )
            m_ref[rho, :, cols] = m_new

    def later_body(n, rho, half, size, kind, masked):
        rows, keys, vis = inputs(n, rho, half, size, kind, masked)
        t_ref[(n * 4 + rho) * 2 + half] = m_ref[rho]
        for p in range(4):
            cols = slice(256 * p, 256 * p + 256)
            e = jnp.exp2((scores(keys, rho, cols, vis) - m_ref[rho, :, cols]) * C2)
            e_ref[n * 4 + rho, rows, cols] = e.astype(BF16)
            sum_ref[rho, :, cols] += jnp.sum(e, axis=0, keepdims=True)

    def attempt(_):
        sum_ref[...] = jnp.zeros_like(sum_ref)
        items(ks, (0, 1, 2, 3), tab, tag_ref, kv, later_body, True, ks[0] != 2)
        sums = sum_ref[...]
        step = jnp.where(sums > 2.0**100, 80.0, jnp.where(sums > 2.0**40, 26.0, 0.0))
        m_ref[...] += step * (1.0 / C2)
        return jnp.max(step)

    if ks == (0,):
        items(ks, (0, 1, 2, 3), tab, tag_ref, kv, first_body, True, False)
    else:
        lax.while_loop(lambda step: step > 0.0, attempt, jnp.float32(1.0))
        l_ref[...] = l_ref[...] * jnp.exp2((refs[3][...] - m_ref[...]) * C2) + sum_ref[...]


def grads_body(ks, rhos, first, last, *refs):
    n_sets = len(ks)
    tab, tag_ref, mean_ref, log_ref, qt_ref, gw_ref, gt_ref, e_ref, t_ref = refs[:9]
    kvs, rest = refs[9 : 9 + n_sets], refs[9 + n_sets :]
    if first:
        dq_ref, acc, kv, p_all, d_all = rest

        def wipe(t):
            dq_ref[:, :, lanes(t)] = jnp.zeros((4, HD, 128), F32)

        each(H, wipe)
    elif last:
        dq_in, pieces, rest = rest[0], rest[1 : 1 + len(rhos)], rest[1 + len(rhos) :]
        acc, kv, p_all, d_all, dq_ref = rest

        def fetch(t):
            dq_ref[:, :, lanes(t)] = dq_in[rhos[0] : rhos[0] + len(rhos), :, lanes(t)]

        each(H, fetch)
    else:
        _, dq_ref, acc, kv, p_all, d_all = rest
    take_sets(kv, kvs)

    def clear(t):
        acc[:, lanes(t), :] = jnp.zeros((n_sets, 128, 2 * HD), F32)

    each(NK // 128, clear)

    def body(n, rho, half, size, kind, masked):
        rows = pl.ds(pl.multiple_of(half * 256, 256), size)
        keys = kv[n, rows, 0:HD]
        vals = kv[n, rows, HD:]
        for p in range(4):
            cols = slice(256 * p, 256 * p + 256)
            dp = dot_nn(vals, gw_ref[rho, :, cols])
            share = jnp.exp2((t_ref[(n * 4 + rho) * 2 + half, :, cols] - log_ref[rho, :, cols]) * C2)
            prob = e_ref[n * 4 + rho, rows, cols].astype(F32) * share
            p_all[0:size, cols] = prob.astype(BF16)
            d_all[0:size, cols] = (prob * (dp - mean_ref[rho, :, cols])).astype(BF16)
        d = d_all[0:size, :]
        acc[n, rows, 0:HD] += dot_nn(d, qt_ref[rho])
        acc[n, rows, HD:] += dot_nn(p_all[0:size, :], gt_ref[rho])
        dq_ref[rho - rhos[0]] += dot_tn(keys, d)

    items(ks, rhos, tab, tag_ref, kv, body, False, not last)
    if last:

        def head(h):
            for r, out in enumerate(pieces):
                out[:, lanes(h)] = (dq_ref[r, :, lanes(h)].T * SCALE).astype(BF16)

        each(H, head)


def place_body(tab, a0, a1, a2, a3, q0, q1, q2, gq_ref, gk_ref, gv_ref):
    col = tab[1]
    for rho, part in enumerate((a0, a1, a2, a3)):
        rows = pl.ds(pl.multiple_of((col ^ rho) * 128, 128), 128)
        gk_ref[rows, :] = part[:, 0:HD]
        gv_ref[rows, :] = part[:, HD:]
    total = q0[...].astype(F32) + q1[...].astype(F32) + q2[...].astype(F32)
    gq_ref[...] = total.astype(BF16)


def per_device(queries, keys, values, grad_out, saved_out, segment_ids, frame_flags):
    hop = functools.partial(lax.ppermute, axis_name="ctx")
    rank = lax.axis_index("ctx").astype(jnp.int32)

    def place_of(rank):
        return jnp.stack([(rank >> 1) & 7, 2 * (rank >> 4) + (rank & 1)])

    tab = place_of(lax.optimization_barrier(rank))
    hbm = pl.BlockSpec(memory_space=pltpu.HBM)

    *parts, q_own = call(
        begin_body, [shape((144, 256))] * 4 + [shape((NQ + 16, H * HD))], [SM] + [hbm] * 5, nbytes=MIB,
        scratch=[
            pltpu.VMEM((NK, HD), BF16), pltpu.VMEM((NK, HD), BF16), pltpu.VMEM((1, NK), jnp.int32),
            pltpu.VMEM((1, 128), jnp.int32), pltpu.SemaphoreType.DMA((5,)),
        ],
        vmem=58,
    )(place_of(rank), keys[0], values[0], segment_ids, frame_flags, queries[0])
    got = [hop(parts[r], perm=flip(r)) for r in (1, 2, 3)]
    own_set = call(join_body, shape((NK + 16, 256)), [VM] * 4, nbytes=MIB)(parts[0], *got)

    def four(x):
        other = hop(x, perm=flip(2))
        last = hop(other, perm=flip(1))
        return (x, hop(x, perm=flip(1)), other, last)

    q_four = four(q_own)
    g_own = call(cotangent_body, shape((NQ + 16, H * HD)), [VM] * 2, nbytes=MIB)(grad_out[0], saved_out[0])
    forms = [shape((4, NQ * H, HD)), shape((4, HD, NQ * H)), shape((4, 1, NQ * H), F32)]

    def turned(four_of, pieces):
        return call(functools.partial(turn_body, pieces), forms, [VM] * 4, vmem=16, nbytes=4 * MIB)(*four_of)

    q_tall, q_wide, tag = turned(q_four, 1)
    stat = shape((4, 1, NQ * H), F32)
    m = jnp.full((4, 1, NQ * H), NEG, F32)
    l = jnp.zeros((4, 1, NQ * H), F32)
    sets = {0: own_set}
    kept = {}
    fwd = bwd = own_set
    for step in range(5):
        ks = (0,) if step == 0 else (4,) if step == 4 else (step, -step)
        n = len(ks)
        if step < 3:
            fwd, bwd = hop(fwd, perm=turn(1)), hop(bwd, perm=turn(-1))
        elif step == 3:
            low, high = hop(fwd[0:272], perm=turn(1)), hop(bwd[272:], perm=turn(-1))
            fwd, bwd = low, high
        m, l, *kept[ks] = call(
            functools.partial(stats_body, ks),
            [stat, stat, shape((4 * n, NK, NQ * H)), shape((8 * n, 1, NQ * H), F32)],
            [SM] + [VM] * (4 + n), vmem=3,
            scratch=[pltpu.VMEM((n, NK + 16, 256), BF16)] + [pltpu.VMEM((4, 1, NQ * H), F32)],
            flops=n * (1 << 29), nbytes=2 * MIB,
        )(tab, tag, q_wide, m, l, *[sets[k] for k in ks])
        if step < 4:
            if step > 0:
                fwd, bwd, m, l = lax.optimization_barrier((fwd, bwd, m, l))
            if step < 3:
                sets[step + 1], sets[-step - 1] = bwd, fwd
            else:
                sets[4] = jnp.concatenate([fwd, bwd], axis=0)
        if step == 0:
            g_four = four(g_own)
    g_tall, g_wide, mean = turned(g_four, 3)

    ml = jnp.concatenate([m, l], axis=0)
    tops, sums = [m], [l]
    for r in (1, 2, 3):
        got = hop(ml, perm=flip(r))
        tops.append(jnp.concatenate([got[rho ^ r : (rho ^ r) + 1] for rho in range(4)], axis=0))
        sums.append(jnp.concatenate([got[4 + (rho ^ r) : 5 + (rho ^ r)] for rho in range(4)], axis=0))
    top = functools.reduce(jnp.maximum, tops)
    total = sum(s * jnp.exp2((t - top) * C2) for s, t in zip(sums, tops))
    log_total = top + jnp.log2(total) * (1.0 / C2)

    dq = None
    up = down = None
    dq_shape = shape((4, HD, NQ * H), F32)

    def grads(ks, rhos, dq):
        n = len(ks)
        first, last = dq is None, ks == (0,)
        args = [tab, tag, mean, log_total, q_tall, g_wide, g_tall, *kept[ks]] + [sets[k] for k in ks]
        args += [] if first else [dq]
        piece = shape((NQ, H * HD))
        scratch = [pltpu.VMEM((n, NK + 16, 256), BF16)] + [pltpu.VMEM((NK, NQ * H), BF16)] * 2
        return call(
            functools.partial(grads_body, ks, rhos, first, last),
            ([piece] * len(rhos) if last else [dq_shape]) + [shape((n, NK, 2 * HD), F32)],
            [SM] + [VM] * (len(args) - 1),
            scratch=scratch + ([pltpu.VMEM((len(rhos), HD, NQ * H), F32)] if last else []),
            vmem=5, flops=n * 5 * (1 << 29), nbytes=8 * MIB,
            alias={} if first or last else {len(args) - 1: 0},
        )(*args)

    for ks in ((4,), (3, -3), (2, -2), (1, -1)):
        n = len(ks)
        dq, adds = grads(ks, (0, 1, 2, 3), dq)
        sends = [(adds[0] if up is None else adds[0] + up.astype(F32)).astype(BF16)]
        if n == 2:
            sends.append((adds[1] if down is None else adds[1] + down.astype(F32)).astype(BF16))
        dq, *sends = lax.optimization_barrier((dq, *sends))
        up = hop(sends[0], perm=turn(1))
        if n == 2:
            down = hop(sends[1], perm=turn(-1))
    dq3, adds3 = grads((0,), (3,), dq)
    dq3 = hop(dq3, perm=flip(1))
    dq2, adds2 = grads((0,), (2,), dq)
    across = (dq2.astype(F32) + dq3.astype(F32)).astype(BF16)
    dq_far = hop(across, perm=flip(2))
    dq0, dq1, adds0 = grads((0,), (0, 1), dq)
    own = adds3[0] + adds2[0] + adds0[0] + up.astype(F32) + down.astype(F32)
    scales = jnp.where(jnp.arange(2 * HD) < HD, SCALE, 1.0).astype(F32)
    own = (own * scales[None, :]).astype(BF16)
    q_back = [dq0, hop(dq1, perm=flip(1)), dq_far]
    a_back = [own[0:128]] + [hop(own[128 * r : 128 * r + 128], perm=flip(r)) for r in (1, 2, 3)]
    gq, gk, gv = call(
        place_body, [shape((NQ, H * HD)), shape((NK, HD)), shape((NK, HD))], [SM] + [VM] * 7,
        nbytes=2 * MIB,
    )(tab, *a_back, *q_back)
    return gq[None], gk[None], gv[None]


def solution(mesh):
    row = P("dp", "ctx", None)
    return jax.shard_map(
        per_device,
        mesh=mesh,
        in_specs=(row, row, row, row, row, P("dp", "ctx"), P("dp", None)),
        out_specs=(row, row, row),
        check_vma=False,
    )
```

```python
import functools
import math

import jax
import jax.numpy as jnp
from jax import lax
from jax.experimental import pallas as pl
from jax.experimental.pallas import tpu as pltpu
from jax.sharding import PartitionSpec as P


H = 8
HD = 128
NQ = 128
NK = 512
NZ = 8
SCALE = 1.0 / math.sqrt(HD)
C2 = SCALE * math.log2(math.e)
NEG = -1e30
F32 = jnp.float32
BF16 = jnp.bfloat16
VM = pl.BlockSpec(memory_space=pltpu.VMEM)
SM = pl.BlockSpec(memory_space=pltpu.SMEM)
MIB = 1 << 20


def flip(rho):
    mask = (rho & 1) | ((rho >> 1) << 4)
    return [(i, i ^ mask) for i in range(32)]


def turn(step):
    return [(i, (i // 16) * 16 + (i % 16 + 2 * step) % 16) for i in range(32)]


def dot_nn(left, right):
    return lax.dot_general(left, right, (((1,), (0,)), ((), ())), preferred_element_type=F32)


def dot_tn(left, right):
    return lax.dot_general(left, right, (((0,), (0,)), ((), ())), preferred_element_type=F32)


def call(body, out, specs, scratch=(), vmem=8, flops=0, nbytes=0, alias=None):
    return pl.pallas_call(
        body,
        out_shape=out,
        in_specs=specs,
        out_specs=jax.tree.map(lambda _: VM, out),
        scratch_shapes=list(scratch),
        input_output_aliases=alias or {},
        cost_estimate=pl.CostEstimate(flops=flops, bytes_accessed=nbytes, transcendentals=0),
        compiler_params=pltpu.CompilerParams(vmem_limit_bytes=vmem * MIB),
    )


def shape(dims, dtype=BF16):
    return jax.ShapeDtypeStruct(dims, dtype)


def each(count, body):
    lax.fori_loop(0, count, lambda t, _: (body(t), 0)[1], 0)


def lanes(t):
    return pl.ds(pl.multiple_of(t * 128, 128), 128)


def take_sets(kv, kvs):
    def rows(t):
        part = pl.ds(pl.multiple_of(t * 48, 16), 48)
        for n in range(len(kvs)):
            kv[n, part, :] = kvs[n][part, :]

    each(11, rows)


def column(row):
    return jnp.broadcast_to(row, (128, 128)).T


def begin_body(tab, k_hbm, v_hbm, seg_hbm, flag_hbm, q_hbm, o0, o1, o2, o3, q_out, k_ref, v_ref, seg_ref, flag_ref, sems):
    moves = [
        pltpu.make_async_copy(source, target, sems.at[n])
        for n, (source, target) in enumerate(
            [(seg_hbm, seg_ref), (flag_hbm, flag_ref), (k_hbm, k_ref), (v_hbm, v_ref), (q_hbm, q_out.at[0:NQ, :])]
        )
    ]
    for move in moves:
        move.start()
    moves[0].wait()
    moves[1].wait()
    own = seg_ref[:, NK - NQ :]
    ident = lax.broadcasted_iota(jnp.int32, (128, 128), 0)
    framed = jnp.sum(jnp.where(ident == own, column(flag_ref[...]), 0), axis=0, keepdims=True)
    tag = jnp.where(framed == 1, own, -1).astype(F32)
    q_out[NQ:, :] = jnp.broadcast_to(jnp.concatenate([tag] * H, axis=1), (16, H * HD)).astype(BF16)
    moves[2].wait()
    moves[3].wait()
    for rho, out in enumerate((o0, o1, o2, o3)):
        first = pl.multiple_of((tab[1] ^ rho) * 128, 128)
        out[0:128, 0:HD] = k_ref[pl.ds(first, 128), :]
        out[0:128, HD:] = v_ref[pl.ds(first, 128), :]
        seg = seg_ref[:, pl.ds(first, 128)].astype(F32)
        out[128:, :] = jnp.broadcast_to(jnp.concatenate([seg, seg], axis=1), (16, 256)).astype(BF16)
    moves[4].wait()


def join_body(p0, p1, p2, p3, out):
    row = lax.broadcasted_iota(jnp.int32, (16, 256), 0)
    seg = jnp.zeros((16, 256), F32)
    for rho, part in enumerate((p0, p1, p2, p3)):
        out[128 * rho : 128 * rho + 128, :] = part[0:128, :]
        seg = jnp.where(row == rho, part[128:, :].astype(F32), seg)
    out[NK:, :] = seg.astype(BF16)


def cotangent_body(g_ref, saved_ref, out_ref):
    out_ref[0:NQ, :] = g_ref[...]
    row = lax.broadcasted_iota(jnp.int32, (16, HD), 0)
    for h in range(H):
        cols = slice(h * HD, h * HD + HD)
        both = g_ref[:, cols].astype(F32) * saved_ref[:, cols].astype(F32)
        mean = jnp.sum(both.T, axis=0, keepdims=True)
        top = mean.astype(BF16).astype(F32)
        mid = (mean - top).astype(BF16).astype(F32)
        low = mean - top - mid
        out_ref[NQ:, cols] = jnp.where(row == 0, top, jnp.where(row == 1, mid, low)).astype(BF16)


def turn_body(pieces, q0, q1, q2, q3, tall_ref, wide_ref, row_ref):
    def head(h):
        for rho, q in enumerate((q0, q1, q2, q3)):
            tile = q[0:NQ, lanes(h)]
            tall_ref[rho, lanes(h), :] = tile
            wide_ref[rho, :, lanes(h)] = tile.astype(F32).T.astype(BF16)

    each(H, head)
    for rho, q in enumerate((q0, q1, q2, q3)):
        extra = q[NQ:, :].astype(F32)
        row = extra[0:1, :]
        for n in range(1, pieces):
            row = row + extra[n : n + 1, :]
        row_ref[rho] = row


def item_kind(tab, z_keys, half, rho):
    z, col = tab[0], tab[1]
    own = col ^ rho
    block = 16 * (own >> 1) + 2 * z + (own & 1)
    b0 = col ^ (2 * half)
    b1 = b0 ^ 1
    p0 = (16 * (b0 >> 1) + 2 * z_keys + (b0 & 1)) * NK + 128 * col
    p1 = (16 * (b1 >> 1) + 2 * z_keys + (b1 & 1)) * NK + 128 * col
    first = block * NK + NK - NQ
    full = jnp.maximum(p0, p1) + 127 <= first
    some = jnp.minimum(p0, p1) <= first + NQ - 1 + 1023
    return p0, p1, first, full, some


def visible_of(kv, n, half, p0, p1, first, tag):
    row = lax.broadcasted_iota(jnp.int32, (128, NQ), 0)
    query = lax.broadcasted_iota(jnp.int32, (128, NQ), 1) + first
    seg = kv[n, NK:, 0:128].astype(F32)
    which = lax.broadcasted_iota(jnp.int32, (16, 128), 0)
    parts = []
    for c, p in enumerate((p0, p1)):
        line = jnp.sum(jnp.where(which == 2 * half + c, seg, 0.0), axis=0, keepdims=True)
        parts.append(jnp.where((p + row <= query) | (column(line) == tag), 1.0, 0.0))
    both = jnp.concatenate(parts, axis=0)
    return jnp.concatenate([both, both], axis=1) > 0.5


def items(ks, rhos, tab, tag_ref, kv, body, masks, wide=True):
    edge = 0 in ks or 1 in ks

    def item(t, _):
        n = t // len(rhos)
        rho = rhos[0] + t % len(rhos)
        k = ks[0] if len(ks) == 1 else jnp.where(n == 0, ks[0], ks[1])
        z_keys = (tab[0] + k + NZ) & (NZ - 1)

        def one(half, _):
            kind = item_kind(tab, z_keys, half, rho)
            p0, p1, first, full, some = kind
            if edge:

                def framed():
                    which = lax.broadcasted_iota(jnp.int32, (16, 128), 0) >> 1
                    least = jnp.min(jnp.where(which == half, kv[n, NK:, 0:128].astype(F32), 1e9))
                    return (least <= jnp.max(tag_ref[rho, :, 0:128])).astype(jnp.int32)

                past = jnp.minimum(p0, p1) > first + NQ - 1
                some = some & (lax.cond(some & past, framed, lambda: jnp.int32(1)) > 0)
                pl.when(full | some)(lambda: body(n, rho, half, NK // 2, kind, masks))
            else:
                pl.when(full)(lambda: body(n, rho, half, NK // 2, kind, False))
            return 0

        if not wide:
            lax.fori_loop(0, 2, one, 0)
        else:
            both = item_kind(tab, z_keys, 0, rho)[3] & item_kind(tab, z_keys, 1, rho)[3]
            pl.when(both)(lambda: body(n, rho, 0, NK, None, False))

            @pl.when(jnp.logical_not(both))
            def _():
                lax.fori_loop(0, 2, one, 0)

        return 0

    lax.fori_loop(0, len(rhos) * len(ks), item, 0)


def stats_body(ks, *refs):
    n_sets = len(ks)
    tab, tag_ref, wide_ref = refs[:3]
    kvs = refs[5 : 5 + n_sets]
    m_ref, l_ref, e_ref, t_ref, kv, sum_ref = refs[5 + n_sets :]
    m_ref[...] = refs[3][...]
    l_ref[...] = refs[4][...]
    take_sets(kv, kvs)

    def inputs(n, rho, half, size, kind, masked):
        rows = pl.ds(pl.multiple_of(half * 256, 256), size)
        vis = visible_of(kv, n, half, *kind[:3], tag_ref[rho, :, 0:128]) if masked else None
        return rows, kv[n, rows, 0:HD], vis

    def scores(keys, rho, cols, vis):
        s = dot_nn(keys, wide_ref[rho, :, cols])
        return s if vis is None else jnp.where(vis, s, NEG)

    def first_body(n, rho, half, size, kind, masked):
        rows, keys, vis = inputs(n, rho, half, size, kind, masked)
        for p in range(4):
            cols = slice(256 * p, 256 * p + 256)
            s = scores(keys, rho, cols, vis)
            m_old = m_ref[rho, :, cols]
            m_new = jnp.maximum(m_old, jnp.max(s, axis=0, keepdims=True))
            e = jnp.exp2((s - m_new) * C2)
            if masked:
                e = jnp.where(vis, e, 0.0)
            e_ref[n * 4 + rho, rows, cols] = e.astype(BF16)
            t_ref[(n * 4 + rho) * 2 + half, :, cols] = m_new
            l_ref[rho, :, cols] = l_ref[rho, :, cols] * jnp.exp2((m_old - m_new) * C2) + jnp.sum(
                e, axis=0, keepdims=True
            )
            m_ref[rho, :, cols] = m_new

    def later_body(n, rho, half, size, kind, masked):
        rows, keys, vis = inputs(n, rho, half, size, kind, masked)
        t_ref[(n * 4 + rho) * 2 + half] = m_ref[rho]
        for p in range(4):
            cols = slice(256 * p, 256 * p + 256)
            e = jnp.exp2((scores(keys, rho, cols, vis) - m_ref[rho, :, cols]) * C2)
            e_ref[n * 4 + rho, rows, cols] = e.astype(BF16)
            sum_ref[rho, :, cols] += jnp.sum(e, axis=0, keepdims=True)

    def attempt(_):
        sum_ref[...] = jnp.zeros_like(sum_ref)
        items(ks, (0, 1, 2, 3), tab, tag_ref, kv, later_body, True)
        sums = sum_ref[...]
        step = jnp.where(sums > 2.0**100, 80.0, jnp.where(sums > 2.0**40, 26.0, 0.0))
        m_ref[...] += step * (1.0 / C2)
        return jnp.max(step)

    if ks == (0,):
        items(ks, (0, 1, 2, 3), tab, tag_ref, kv, first_body, True, False)
    else:
        lax.while_loop(lambda step: step > 0.0, attempt, jnp.float32(1.0))
        l_ref[...] = l_ref[...] * jnp.exp2((refs[3][...] - m_ref[...]) * C2) + sum_ref[...]


def grads_body(ks, rhos, first, last, *refs):
    n_sets = len(ks)
    tab, tag_ref, mean_ref, log_ref, qt_ref, gw_ref, gt_ref, e_ref, t_ref = refs[:9]
    kvs, rest = refs[9 : 9 + n_sets], refs[9 + n_sets :]
    if first:
        dq_ref, acc, kv, p_all, d_all = rest

        def wipe(t):
            dq_ref[:, :, lanes(t)] = jnp.zeros((4, HD, 128), F32)

        each(H, wipe)
    elif last:
        dq_in, pieces, rest = rest[0], rest[1 : 1 + len(rhos)], rest[1 + len(rhos) :]
        acc, kv, p_all, d_all, dq_ref = rest

        def fetch(t):
            dq_ref[:, :, lanes(t)] = dq_in[rhos[0] : rhos[0] + len(rhos), :, lanes(t)]

        each(H, fetch)
    else:
        _, dq_ref, acc, kv, p_all, d_all = rest
    take_sets(kv, kvs)

    def clear(t):
        acc[:, lanes(t), :] = jnp.zeros((n_sets, 128, 2 * HD), F32)

    each(NK // 128, clear)

    def body(n, rho, half, size, kind, masked):
        rows = pl.ds(pl.multiple_of(half * 256, 256), size)
        keys = kv[n, rows, 0:HD]
        vals = kv[n, rows, HD:]
        for p in range(4):
            cols = slice(256 * p, 256 * p + 256)
            dp = dot_nn(vals, gw_ref[rho, :, cols])
            share = jnp.exp2((t_ref[(n * 4 + rho) * 2 + half, :, cols] - log_ref[rho, :, cols]) * C2)
            prob = e_ref[n * 4 + rho, rows, cols].astype(F32) * share
            p_all[0:size, cols] = prob.astype(BF16)
            d_all[0:size, cols] = (prob * (dp - mean_ref[rho, :, cols])).astype(BF16)
        d = d_all[0:size, :]
        acc[n, rows, 0:HD] += dot_nn(d, qt_ref[rho])
        acc[n, rows, HD:] += dot_nn(p_all[0:size, :], gt_ref[rho])
        dq_ref[rho - rhos[0]] += dot_tn(keys, d)

    items(ks, rhos, tab, tag_ref, kv, body, False, not last)
    if last:

        def head(h):
            for r, out in enumerate(pieces):
                out[:, lanes(h)] = (dq_ref[r, :, lanes(h)].T * SCALE).astype(BF16)

        each(H, head)


def place_body(tab, a0, a1, a2, a3, q0, q1, q2, gq_ref, gk_ref, gv_ref):
    col = tab[1]
    for rho, part in enumerate((a0, a1, a2, a3)):
        rows = pl.ds(pl.multiple_of((col ^ rho) * 128, 128), 128)
        gk_ref[rows, :] = part[:, 0:HD]
        gv_ref[rows, :] = part[:, HD:]
    total = q0[...].astype(F32) + q1[...].astype(F32) + q2[...].astype(F32)
    gq_ref[...] = total.astype(BF16)


def per_device(queries, keys, values, grad_out, saved_out, segment_ids, frame_flags):
    hop = functools.partial(lax.ppermute, axis_name="ctx")
    rank = lax.axis_index("ctx").astype(jnp.int32)

    def place_of(rank):
        return jnp.stack([(rank >> 1) & 7, 2 * (rank >> 4) + (rank & 1)])

    tab = place_of(lax.optimization_barrier(rank))
    hbm = pl.BlockSpec(memory_space=pltpu.HBM)

    *parts, q_own = call(
        begin_body, [shape((144, 256))] * 4 + [shape((NQ + 16, H * HD))], [SM] + [hbm] * 5, nbytes=MIB,
        scratch=[
            pltpu.VMEM((NK, HD), BF16), pltpu.VMEM((NK, HD), BF16), pltpu.VMEM((1, NK), jnp.int32),
            pltpu.VMEM((1, 128), jnp.int32), pltpu.SemaphoreType.DMA((5,)),
        ],
        vmem=58,
    )(place_of(rank), keys[0], values[0], segment_ids, frame_flags, queries[0])
    got = [hop(parts[r], perm=flip(r)) for r in (1, 2, 3)]
    own_set = call(join_body, shape((NK + 16, 256)), [VM] * 4, nbytes=MIB)(parts[0], *got)

    def four(x):
        other = hop(x, perm=flip(2))
        last = hop(other, perm=flip(1))
        return (x, hop(x, perm=flip(1)), other, last)

    q_four = four(q_own)
    g_own = call(cotangent_body, shape((NQ + 16, H * HD)), [VM] * 2, nbytes=MIB)(grad_out[0], saved_out[0])
    forms = [shape((4, NQ * H, HD)), shape((4, HD, NQ * H)), shape((4, 1, NQ * H), F32)]

    def turned(four_of, pieces):
        return call(functools.partial(turn_body, pieces), forms, [VM] * 4, vmem=16, nbytes=4 * MIB)(*four_of)

    q_tall, q_wide, tag = turned(q_four, 1)
    stat = shape((4, 1, NQ * H), F32)
    m = jnp.full((4, 1, NQ * H), NEG, F32)
    l = jnp.zeros((4, 1, NQ * H), F32)
    sets = {0: own_set}
    kept = {}
    fwd = bwd = own_set
    for step in range(5):
        ks = (0,) if step == 0 else (4,) if step == 4 else (step, -step)
        n = len(ks)
        if step < 3:
            fwd, bwd = hop(fwd, perm=turn(1)), hop(bwd, perm=turn(-1))
        elif step == 3:
            low, high = hop(fwd[0:272], perm=turn(1)), hop(bwd[272:], perm=turn(-1))
            fwd, bwd = low, high
        m, l, *kept[ks] = call(
            functools.partial(stats_body, ks),
            [stat, stat, shape((4 * n, NK, NQ * H)), shape((8 * n, 1, NQ * H), F32)],
            [SM] + [VM] * (4 + n), vmem=3,
            scratch=[pltpu.VMEM((n, NK + 16, 256), BF16)] + [pltpu.VMEM((4, 1, NQ * H), F32)],
            flops=n * (1 << 29), nbytes=2 * MIB,
        )(tab, tag, q_wide, m, l, *[sets[k] for k in ks])
        if step < 4:
            if step > 0:
                fwd, bwd, m, l = lax.optimization_barrier((fwd, bwd, m, l))
            if step < 3:
                sets[step + 1], sets[-step - 1] = bwd, fwd
            else:
                sets[4] = jnp.concatenate([fwd, bwd], axis=0)
        if step == 0:
            g_four = four(g_own)
    g_tall, g_wide, mean = turned(g_four, 3)

    ml = jnp.concatenate([m, l], axis=0)
    tops, sums = [m], [l]
    for r in (1, 2, 3):
        got = hop(ml, perm=flip(r))
        tops.append(jnp.concatenate([got[rho ^ r : (rho ^ r) + 1] for rho in range(4)], axis=0))
        sums.append(jnp.concatenate([got[4 + (rho ^ r) : 5 + (rho ^ r)] for rho in range(4)], axis=0))
    top = functools.reduce(jnp.maximum, tops)
    total = sum(s * jnp.exp2((t - top) * C2) for s, t in zip(sums, tops))
    log_total = top + jnp.log2(total) * (1.0 / C2)

    dq = None
    up = down = None
    dq_shape = shape((4, HD, NQ * H), F32)

    def grads(ks, rhos, dq):
        n = len(ks)
        first, last = dq is None, ks == (0,)
        args = [tab, tag, mean, log_total, q_tall, g_wide, g_tall, *kept[ks]] + [sets[k] for k in ks]
        args += [] if first else [dq]
        piece = shape((NQ, H * HD))
        scratch = [pltpu.VMEM((n, NK + 16, 256), BF16)] + [pltpu.VMEM((NK, NQ * H), BF16)] * 2
        return call(
            functools.partial(grads_body, ks, rhos, first, last),
            ([piece] * len(rhos) if last else [dq_shape]) + [shape((n, NK, 2 * HD), F32)],
            [SM] + [VM] * (len(args) - 1),
            scratch=scratch + ([pltpu.VMEM((len(rhos), HD, NQ * H), F32)] if last else []),
            vmem=5, flops=n * 5 * (1 << 29), nbytes=8 * MIB,
            alias={} if first or last else {len(args) - 1: 0},
        )(*args)

    for ks in ((4,), (3, -3), (2, -2), (1, -1)):
        n = len(ks)
        dq, adds = grads(ks, (0, 1, 2, 3), dq)
        sends = [(adds[0] if up is None else adds[0] + up.astype(F32)).astype(BF16)]
        if n == 2:
            sends.append((adds[1] if down is None else adds[1] + down.astype(F32)).astype(BF16))
        dq, *sends = lax.optimization_barrier((dq, *sends))
        up = hop(sends[0], perm=turn(1))
        if n == 2:
            down = hop(sends[1], perm=turn(-1))
    *dq_four, adds0 = grads((0,), (0, 1, 2, 3), dq)
    dq3 = hop(dq_four[3], perm=flip(1))
    own = adds0[0] + up.astype(F32) + down.astype(F32)
    scales = jnp.where(jnp.arange(2 * HD) < HD, SCALE, 1.0).astype(F32)
    own = (own * scales[None, :]).astype(BF16)
    a_back = [own[0:128]] + [hop(own[128 * r : 128 * r + 128], perm=flip(r)) for r in (1, 2, 3)]
    across = (dq_four[2].astype(F32) + dq3.astype(F32)).astype(BF16)
    dq_far = hop(across, perm=flip(2))
    q_back = [dq_four[0], hop(dq_four[1], perm=flip(1)), dq_far]
    gq, gk, gv = call(
        place_body, [shape((NQ, H * HD)), shape((NK, HD)), shape((NK, HD))], [SM] + [VM] * 7,
        nbytes=2 * MIB,
    )(tab, *a_back, *q_back)
    return gq[None], gk[None], gv[None]


def solution(mesh):
    row = P("dp", "ctx", None)
    return jax.shard_map(
        per_device,
        mesh=mesh,
        in_specs=(row, row, row, row, row, P("dp", "ctx"), P("dp", None)),
        out_specs=(row, row, row),
        check_vma=False,
    )
```
